512 devices in a mesh: ctx: 64 (over y, x, z_hi), dp: 8 (over z_lo, core).
Axes of the slice: x: 4, y: 8, z: 8 (z_hi: 2, z_lo: 4; z = z_hi * 4 + z_lo), core: 2. Of those that a mesh axis runs over, the one named last changes fastest.
Arguments:
- query_rows: bfloat16 [131072, 1024], P(('dp', 'ctx')), parts along dimension 0, may hold values from -100 to 100
- key_rows: bfloat16 [131072, 1024], P(('dp', 'ctx')), parts along dimension 0, may hold values from -5 to 5
- value_rows: bfloat16 [131072, 1024], P(('dp', 'ctx')), parts along dimension 0, may hold values from -6 to 6
- channels: bfloat16 [131072, 2048], P(('dp', 'ctx')), parts along dimension 0, may hold values from -6 to 6
- step_low: bfloat16 [131072, 128], P(('dp', 'ctx')), parts along dimension 0, may hold values from -6 to 6
- step_proj: bfloat16 [128, 2048], replicated, may hold values from -0.5 to 0.5
- step_bias: float32 [2048], replicated, may hold values from -8 to -2.5
- decay_log: float32 [16, 2048], replicated, may hold values from -6.5 to -0.5
- state_maps: float32 [2, 16, 131072], P(None, None, ('dp', 'ctx')), parts along dimension 2, may hold values from -6 to 6
- attend_weight: bfloat16 [1024, 128], replicated, may hold values from -0.5 to 0.5
- mixer_weight: bfloat16 [2048, 128], replicated, may hold values from -0.125 to 0.125
Outputs:
- token_vectors: bfloat16 [131072, 128], P(('dp', 'ctx')), parts along dimension 0
The draws below stay inside these ranges and needn't reach their ends.
There are 8 independent parts, one for each index of `dp`. The reference program is written for one: setup_inputs(seed, part) draws one part's arguments, and reference() takes and returns one part's arrays. A program takes and returns all parts, laid end to end along the dimension named above; an argument that names none is the same for every part. Nothing has to cross between parts.
All inputs are finite; a program needn't handle non-finite values.
Results may differ from the reference program's by a relative error of at most 0.005.
Values may be sent and summed in bfloat16 or wider, within the bound.
No kernel may reach another device: no remote copies, remote signals or barrier semaphores. Data moves between devices by JAX's collectives and lax.ppermute only.
A program may use at most 128 MiB of HBM per device.

```python
import math
import jax
import jax.numpy as jnp
from jax import lax

HEADS = 8
HD = 128
CH = 2048
NS = 16
RANK = 128
EMB = 128
TOK_DEV = 256
SEQ = 16384
N_CTX = 64


def attention_pair(key):
    splits = jax.random.split(key, 2)
    feature_count = HEADS * HD
    query_base = jnp.clip(jax.random.normal(splits[0], (SEQ, feature_count), jnp.float32) * 1.2, -4.8, 4.8)
    key_base = jnp.clip(jax.random.normal(splits[1], (SEQ, feature_count), jnp.float32) * 1.2, -4.8, 4.8)
    return (query_base, key_base)


def draw_query_rows(key, part):
    return attention_pair(jax.random.fold_in(key, 11))[0].astype(jnp.bfloat16)


def draw_key_rows(key, part):
    return attention_pair(jax.random.fold_in(key, 11))[1].astype(jnp.bfloat16)


def mixer_rates(key):
    splits = jax.random.split(key, 4)
    share = 0.5
    slow_mask = jax.random.uniform(splits[0], (CH,), jnp.float32) < share
    slow_target = jnp.exp(jax.random.uniform(splits[1], (CH,), jnp.float32, math.log(0.2), math.log(2.0))) / SEQ
    fast_target = jnp.exp(jax.random.uniform(splits[2], (CH,), jnp.float32, math.log(0.1 / TOK_DEV), math.log(1.0 / 35.0)))
    target = jnp.where(slow_mask, slow_target, fast_target)
    spread = jnp.exp(jax.random.uniform(splits[3], (NS, CH), jnp.float32, math.log(0.6), math.log(1.6)))
    bias = jnp.log(0.5 * jnp.sqrt(target)) - 0.5
    rates = 2.0 * jnp.sqrt(target)[None, :] * spread
    return (bias, jnp.log(rates))


def draw_step_bias(key, part):
    return mixer_rates(jax.random.fold_in(key, 23))[0]


def draw_decay_log(key, part):
    return mixer_rates(jax.random.fold_in(key, 23))[1]


def shard_levels(rng, shape, cuts, low, high):
    def one(position, blocks):
        draws = jax.random.uniform(jax.random.fold_in(jax.random.fold_in(rng, 6), position), (blocks,), jnp.float32, low / len(cuts), high / len(cuts))
        return jnp.repeat(jnp.exp(draws), shape[position] // blocks).reshape((-1,) + (1,) * (len(shape) - position - 1))

    factor_of = one(*cuts[0])
    for cut in cuts[1:]:
        factor_of = factor_of * one(*cut)
    return factor_of


def gaussian(rng, extent, deviation, limit, cuts=(), held_as=jnp.bfloat16):
    values = deviation * jax.random.normal(rng, extent, jnp.float32)
    if cuts:
        values = values * shard_levels(rng, extent, cuts, -0.22, 0.18)
    return jnp.clip(values, -limit, limit).astype(held_as)


def setup_inputs(seed: int = 0, part: int = 0) -> dict:
    seeds = jax.random.split(jax.random.key(seed), 12)
    own_keys = jax.random.split(jax.random.fold_in(seeds[11], part), 12)
    return {
        "query_rows": draw_query_rows(jax.random.fold_in(jax.random.fold_in(seeds[11], part), 71), part),
        "key_rows": draw_key_rows(jax.random.fold_in(jax.random.fold_in(seeds[11], part), 71), part),
        "value_rows": gaussian(own_keys[2], (SEQ, HEADS * HD), 1.0, 6.0, ((0, 64),)),
        "channels": gaussian(own_keys[3], (SEQ, CH), 1.0, 6.0, ((0, 64),)),
        "step_low": gaussian(own_keys[4], (SEQ, RANK), 1.0, 6.0, ((0, 64),)),
        "step_proj": gaussian(seeds[5], (RANK, CH), RANK ** -0.5, 0.5),
        "step_bias": draw_step_bias(jax.random.fold_in(seeds[11], 71), part),
        "decay_log": draw_decay_log(jax.random.fold_in(seeds[11], 71), part),
        "state_maps": gaussian(own_keys[8], (2, NS, SEQ), 1.0, 6.0, ((2, 64),), jnp.float32),
        "attend_weight": gaussian(seeds[9], (HEADS * HD, EMB), HD ** -0.5, 0.5),
        "mixer_weight": gaussian(seeds[10], (CH, EMB), CH ** -0.5, 0.125),
    }


def attend_all(query_rows, key_rows, value_rows):
    feature_count = query_rows.shape[1]
    head_count = feature_count // HD
    window_rows = 4 * TOK_DEV
    pad_keys = jnp.concatenate([jnp.zeros((window_rows, feature_count), key_rows.dtype), key_rows], 0)
    pad_values = jnp.concatenate([jnp.zeros((window_rows, feature_count), value_rows.dtype), value_rows], 0)
    query_pos = jnp.arange(TOK_DEV, dtype=jnp.int32)[:, None]
    column = jnp.arange(5 * TOK_DEV, dtype=jnp.int32)[None, :]
    offset = column - window_rows
    base_mask = (offset <= query_pos) & (query_pos - offset < window_rows)

    def one_block(block_index):
        first_row = (block_index * TOK_DEV).astype(jnp.int32)
        query_block = lax.dynamic_slice_in_dim(query_rows, first_row, TOK_DEV, 0).astype(jnp.float32).reshape(TOK_DEV, head_count, HD)
        key_block = lax.dynamic_slice_in_dim(pad_keys, first_row, 5 * TOK_DEV, 0).astype(jnp.float32).reshape(5 * TOK_DEV, head_count, HD)
        value_block = lax.dynamic_slice_in_dim(pad_values, first_row, 5 * TOK_DEV, 0).astype(jnp.float32).reshape(5 * TOK_DEV, head_count, HD)
        scores = jnp.einsum('qhd,khd->hqk', query_block, key_block) * (1.0 / math.sqrt(HD))
        allowed = base_mask & (first_row + offset >= 0)
        scores = jnp.where(allowed[None], scores, -1e+30)
        row_max = lax.optimization_barrier(jnp.max(scores, -1, keepdims=True))
        exp_terms = jnp.exp(scores - row_max)
        row_sum = lax.optimization_barrier(jnp.sum(exp_terms, -1))
        rounded = lax.optimization_barrier(exp_terms.astype(jnp.bfloat16))
        weights = rounded.astype(jnp.float32)
        summed = jnp.einsum('hqk,khd->qhd', weights, value_block)
        result = summed / jnp.transpose(row_sum)[:, :, None]
        return result.reshape(TOK_DEV, feature_count).astype(jnp.bfloat16)
    blocks = lax.map(one_block, jnp.arange(N_CTX, dtype=jnp.int32))
    return blocks.reshape(SEQ, feature_count)

def mixer_all(channels, step_low, step_proj, step_bias, decay_log, state_maps):
    timestep = jax.nn.softplus(jnp.dot(step_low, step_proj, preferred_element_type=jnp.float32) + step_bias)
    decay_rate = -jnp.exp(decay_log)
    inflow = timestep * channels.astype(jnp.float32)

    def advance(carry_state, inputs):
        step_row, inflow_row, in_row, out_row = inputs
        carry_state = jnp.exp(step_row[None, :] * decay_rate) * carry_state + in_row[:, None] * inflow_row[None, :]
        return (carry_state, lax.optimization_barrier(jnp.sum(out_row[:, None] * carry_state, 0)))
    zero_state = jnp.zeros(decay_log.shape, jnp.float32)
    final_state, outputs = lax.scan(advance, zero_state, (timestep, inflow, jnp.transpose(state_maps[0]), jnp.transpose(state_maps[1])))
    return outputs

def reference(query_rows, key_rows, value_rows, channels, step_low, step_proj, step_bias, decay_log, state_maps, attend_weight, mixer_weight):
    mixer_out = mixer_all(channels, step_low, step_proj, step_bias, decay_log, state_maps)
    mixer_norm = (mixer_out * lax.rsqrt(lax.optimization_barrier(jnp.mean(mixer_out * mixer_out, -1, keepdims=True)) + 1e-05)).astype(jnp.bfloat16)
    attended = attend_all(query_rows, key_rows, value_rows)
    combined = jnp.dot(attended, attend_weight, preferred_element_type=jnp.float32) + jnp.dot(mixer_norm, mixer_weight, preferred_element_type=jnp.float32)
    return (combined * lax.rsqrt(lax.optimization_barrier(jnp.mean(combined * combined, -1, keepdims=True)) + 1e-06)).astype(jnp.bfloat16)
```

```python
import math

import jax
import jax.numpy as jnp
from jax import lax
from jax.experimental import pallas as pl
from jax.experimental.pallas import tpu as pltpu
from jax.sharding import PartitionSpec as P

HD = 128
HEADS = 8
TOK = 256
NS = 16
CH = 2048
EMB = 128
CW = 512
LANES = 128
BLK = 16
N_CTX = 64
LOG2E = 1.4426950408889634
SCALE2 = LOG2E / math.sqrt(HD)
F32 = jnp.float32
BF16 = jnp.bfloat16


def dot(a, b):
    return jnp.dot(a, b, preferred_element_type=F32)


def dot_t(a, b):
    return lax.dot_general(a, b, (((1,), (1,)), ((), ())), preferred_element_type=F32)


def pieces(x):
    hi = x.astype(BF16)
    rest = x - hi.astype(F32)
    mid = rest.astype(BF16)
    low = (rest - mid.astype(F32)).astype(BF16)
    return hi, mid, low


def mixer_kernel(
    low_ref, proj_ref, bias_ref, chan_ref, log_ref, maps_ref,
    y_ref, cum_ref, send_ref, out_hi_ref, out_lo_ref,
    step_s, flow_s, in_s, hist,
):
    groups = CW // LANES

    @pl.when(pl.program_id(0) == 0)
    def _():
        in_map = maps_ref[0]
        for t in range(TOK):
            in_s[t] = jnp.broadcast_to(in_map[:, t : t + 1], (NS, LANES))
        spread = (
            lax.broadcasted_iota(jnp.int32, (NS, BLK * NS), 1) % NS
            == lax.broadcasted_iota(jnp.int32, (NS, BLK * NS), 0)
        ).astype(F32).astype(BF16)
        keep = (
            lax.broadcasted_iota(jnp.int32, (TOK, BLK * NS), 1) // NS
            == lax.broadcasted_iota(jnp.int32, (TOK, BLK * NS), 0) % BLK
        )
        hi, mid, _ = pieces(jnp.transpose(maps_ref[1]))
        out_hi_ref[...] = jnp.where(keep, dot(hi, spread), 0.0).astype(BF16)
        out_lo_ref[...] = jnp.where(keep, dot(mid, spread), 0.0).astype(BF16)

    step = jax.nn.softplus(dot(low_ref[...], proj_ref[...]) + bias_ref[...])
    step_s[...] = step.reshape(TOK // BLK, BLK, CW)
    flow_s[...] = (step * chan_ref[...].astype(F32)).reshape(TOK // BLK, BLK, CW)
    triangle = (
        lax.broadcasted_iota(jnp.int32, (TOK, TOK), 0)
        >= lax.broadcasted_iota(jnp.int32, (TOK, TOK), 1)
    ).astype(F32).astype(BF16)
    hi, mid, low = pieces(step)
    cum = dot(triangle, hi) + dot(triangle, mid) + dot(triangle, low)
    cum_ref[...] = cum.reshape(TOK // BLK, BLK, CW)
    rate = -jnp.exp(log_ref[...]) * LOG2E
    rates = [rate[:, g * LANES : (g + 1) * LANES] for g in range(groups)]

    def block(j, states):
        states = list(states)
        for t in range(BLK):
            gain = in_s[j * BLK + t]
            for g in range(groups):
                lanes = slice(g * LANES, (g + 1) * LANES)
                decay = jnp.exp2(step_s[j, t : t + 1, lanes] * rates[g])
                states[g] = decay * states[g] + gain * flow_s[j, t : t + 1, lanes]
                hist[t * NS : (t + 1) * NS, lanes] = states[g].astype(BF16)
        rows = pl.ds(pl.multiple_of(j * BLK, BLK), BLK)
        past = hist[...]
        y_ref[j] = dot(out_hi_ref[rows, :], past) + dot(out_lo_ref[rows, :], past)
        return tuple(states)

    states = lax.fori_loop(
        0, TOK // BLK, block, tuple(jnp.zeros((NS, LANES), F32) for _ in range(groups))
    )
    total = cum[TOK - 1 : TOK, :]
    hi, mid, low = (v.astype(F32) for v in pieces(total))
    for g in range(groups):
        lanes = slice(g * LANES, (g + 1) * LANES)
        for k in range(NS // 4):
            send_ref[g * 4 + k] = jnp.concatenate(
                [
                    states[g][4 * k : 4 * k + 4, :], hi[:, lanes], mid[:, lanes], low[:, lanes],
                    jnp.zeros((1, LANES), F32),
                ],
                0,
            ).astype(BF16)


def run_mixer(step_low, step_proj, step_bias, channels, decay_log, state_maps):
    blocked = (TOK // BLK, BLK, CW)
    whole = jax.ShapeDtypeStruct((TOK // BLK, BLK, CH), F32)
    square = jax.ShapeDtypeStruct((TOK, BLK * NS), BF16)
    fixed = lambda shape: pl.BlockSpec(shape, lambda i: (0,) * len(shape))
    return pl.pallas_call(
        mixer_kernel,
        grid=(CH // CW,),
        in_specs=[
            fixed((TOK, 128)),
            pl.BlockSpec((128, CW), lambda i: (0, i)),
            pl.BlockSpec((1, CW), lambda i: (0, i)),
            pl.BlockSpec((TOK, CW), lambda i: (0, i)),
            pl.BlockSpec((NS, CW), lambda i: (0, i)),
            fixed((2, NS, TOK)),
        ],
        out_specs=[
            pl.BlockSpec(blocked, lambda i: (0, 0, i)),
            pl.BlockSpec(blocked, lambda i: (0, 0, i)),
            pl.BlockSpec((CW // LANES * 4, 8, LANES), lambda i: (i, 0, 0)),
            fixed((TOK, BLK * NS)),
            fixed((TOK, BLK * NS)),
        ],
        out_shape=[whole, whole, jax.ShapeDtypeStruct((N_CTX, 8, LANES), BF16), square, square],
        scratch_shapes=[
            pltpu.VMEM(blocked, F32),
            pltpu.VMEM(blocked, F32),
            pltpu.VMEM((TOK, NS, LANES), F32),
            pltpu.VMEM((BLK * NS, CW), BF16),
        ],
        cost_estimate=pl.CostEstimate(
            flops=6_000_000_000, bytes_accessed=8 << 20, transcendentals=8 << 20
        ),
        name="mixer",
    )(step_low, step_proj, step_bias.reshape(1, CH), channels, decay_log, state_maps)


def prefix_kernel(pos_ref, got_ref, log_ref, out_ref):
    part = lax.rem(pos_ref[0], 4)
    rates = -jnp.exp(log_ref[...]) * LOG2E
    rate = rates[0:4]
    for k in range(1, 4):
        rate = jnp.where(part == k, rates[4 * k : 4 * k + 4], rate)
    state = jnp.zeros((4, LANES), F32)
    for s in range(N_CTX):
        out_ref[s] = state
        got = got_ref[s].astype(F32)
        total = got[4:5] + got[5:6] + got[6:7]
        state = jnp.exp2(rate * total) * state + got[0:4]


def run_prefix(position, got, decay_log):
    return pl.pallas_call(
        prefix_kernel,
        grid_spec=pltpu.PrefetchScalarGridSpec(
            num_scalar_prefetch=1,
            grid=(1,),
            in_specs=[
                pl.BlockSpec((N_CTX, 8, LANES), lambda i, pos: (0, 0, 0)),
                pl.BlockSpec((NS, LANES), lambda i, pos: (0, pos[0] // 4)),
            ],
            out_specs=pl.BlockSpec((N_CTX, 4, LANES), lambda i, pos: (0, 0, 0)),
        ),
        out_shape=jax.ShapeDtypeStruct((N_CTX, 4, LANES), F32),
        cost_estimate=pl.CostEstimate(flops=1 << 20, bytes_accessed=1 << 18, transcendentals=1 << 15),
        name="prefix",
    )(position, got, decay_log)


def finish_kernel(
    y_ref, cum_ref, enter_ref, log_ref, out_hi_ref, out_lo_ref, own_ref, back_ref, weight_ref,
    o_ref, hist, total_s,
):
    groups = CW // LANES
    i = pl.program_id(0)
    rate = -jnp.exp(log_ref[...]) * LOG2E
    rates = [rate[:, g * LANES : (g + 1) * LANES] for g in range(groups)]
    enter = [
        jnp.concatenate([enter_ref[g * 4 + k] for k in range(4)], 0) for g in range(groups)
    ]

    def block(j, carry):
        for t in range(BLK):
            for g in range(groups):
                lanes = slice(g * LANES, (g + 1) * LANES)
                decay = jnp.exp2(cum_ref[j, t : t + 1, lanes] * rates[g])
                hist[t * NS : (t + 1) * NS, lanes] = (decay * enter[g]).astype(BF16)
        rows = pl.ds(pl.multiple_of(j * BLK, BLK), BLK)
        past = hist[...]
        total_s[i, rows, :] = (
            y_ref[j] + dot(out_hi_ref[rows, :], past) + dot(out_lo_ref[rows, :], past)
        )
        return carry

    lax.fori_loop(0, TOK // BLK, block, 0)

    @pl.when(i == CH // CW - 1)
    def _():
        square = jnp.zeros((TOK, 1), F32)
        for k in range(CH // CW):
            square += jnp.sum(total_s[k] * total_s[k], -1, keepdims=True)
        inverse = lax.rsqrt(square * (1.0 / CH) + 1e-05)
        combined = own_ref[...] + back_ref[...].astype(F32)
        for k in range(CH // CW):
            combined += dot(
                (total_s[k] * inverse).astype(BF16), weight_ref[k * CW : (k + 1) * CW, :]
            )
        mean = jnp.mean(combined * combined, -1, keepdims=True)
        o_ref[...] = (combined * lax.rsqrt(mean + 1e-06)).astype(BF16)


def run_finish(y, cum, enter, decay_log, out_hi, out_lo, own, back, mixer_weight):
    blocked = pl.BlockSpec((TOK // BLK, BLK, CW), lambda i: (0, 0, i))
    fixed = lambda shape: pl.BlockSpec(shape, lambda i: (0,) * len(shape))
    return pl.pallas_call(
        finish_kernel,
        grid=(CH // CW,),
        in_specs=[
            blocked,
            blocked,
            pl.BlockSpec((CW // LANES * 4, 4, LANES), lambda i: (i, 0, 0)),
            pl.BlockSpec((NS, CW), lambda i: (0, i)),
            fixed((TOK, BLK * NS)),
            fixed((TOK, BLK * NS)),
            fixed((TOK, EMB)),
            fixed((TOK, EMB)),
            fixed((CH, EMB)),
        ],
        out_specs=fixed((TOK, EMB)),
        out_shape=jax.ShapeDtypeStruct((TOK, EMB), BF16),
        scratch_shapes=[
            pltpu.VMEM((BLK * NS, CW), BF16),
            pltpu.VMEM((CH // CW, TOK, CW), F32),
        ],
        cost_estimate=pl.CostEstimate(
            flops=4_000_000_000, bytes_accessed=6 << 20, transcendentals=8 << 20
        ),
        name="finish",
    )(y, cum, enter, decay_log, out_hi, out_lo, own, back, mixer_weight)


def scores_kernel(pos_ref, q_ref, p_ref, k0_ref, k1_ref, k2_ref, w_ref, stat_ref, table):
    h = pl.program_id(0)
    side = lax.rem(pos_ref[0], 2)
    pair = pos_ref[0] // 2
    gone1 = jnp.where(pair >= 1, 0.0, -1e30).astype(F32)
    gone2 = jnp.where(pair >= 2, 0.0, -1e30).astype(F32)
    row = lax.broadcasted_iota(jnp.int32, (TOK, TOK), 0)
    column = lax.broadcasted_iota(jnp.int32, (TOK, TOK), 1)
    lane = lax.broadcasted_iota(jnp.int32, (TOK, LANES), 1)
    k0, k1, k2 = k0_ref[...], k1_ref[...], k2_ref[...]

    @pl.when(h == 0)
    def _():
        table[...] = jnp.zeros_like(table)

    def weigh(blocks, first, slot):
        top = blocks[0][1] + jnp.max(blocks[0][0], -1, keepdims=True)
        for score, gone in blocks[1:]:
            top = jnp.maximum(top, gone + jnp.max(score, -1, keepdims=True))
        total = jnp.zeros((TOK, 1), F32)
        for n, (score, gone) in enumerate(blocks):
            terms = jnp.exp2(score - (top - gone))
            total += jnp.sum(terms, -1, keepdims=True)
            w_ref[0, :, (first + n) * TOK : (first + n + 1) * TOK] = terms.astype(BF16)
        now = table[...]
        now = jnp.where(lane == slot + h, top, now)
        table[...] = jnp.where(lane == slot + HEADS + h, total, now)

    q = q_ref[...]
    weigh(
        [
            (jnp.where(column <= row, dot_t(q, k0) * SCALE2, -1e30), jnp.float32(0.0)),
            (dot_t(q, k1) * SCALE2, gone1),
            (jnp.where(column > row, dot_t(q, k2) * SCALE2, -1e30), gone2),
        ],
        0,
        0,
    )
    other = p_ref[...]
    ka = jnp.where(side == 0, k0, k1)
    kb = jnp.where(side == 0, k1, k2)
    weigh(
        [
            (dot_t(other, ka) * SCALE2, jnp.where(side == 0, 0.0, gone1)),
            (dot_t(other, kb) * SCALE2, jnp.where(side == 0, gone1, gone2)),
        ],
        3,
        2 * HEADS,
    )

    @pl.when(h == HEADS - 1)
    def _():
        stat_ref[...] = jnp.transpose(table[...])[: 4 * HEADS, :]


def run_scores(position, query, other, k0, k1, k2):
    head = pl.BlockSpec((TOK, HD), lambda h, pos: (0, h))
    return pl.pallas_call(
        scores_kernel,
        grid_spec=pltpu.PrefetchScalarGridSpec(
            num_scalar_prefetch=1,
            grid=(HEADS,),
            in_specs=[head] * 5,
            out_specs=[
                pl.BlockSpec((1, TOK, 5 * TOK), lambda h, pos: (h, 0, 0)),
                pl.BlockSpec((4 * HEADS, TOK), lambda h, pos: (0, 0)),
            ],
            scratch_shapes=[pltpu.VMEM((TOK, LANES), F32)],
        ),
        out_shape=[
            jax.ShapeDtypeStruct((HEADS, TOK, 5 * TOK), BF16),
            jax.ShapeDtypeStruct((4 * HEADS, TOK), F32),
        ],
        cost_estimate=pl.CostEstimate(
            flops=700_000_000, bytes_accessed=8 << 20, transcendentals=3 << 20
        ),
        name="scores",
    )(position, query, other, k0, k1, k2)


def values_kernel(
    pos_ref, w_ref, v0_ref, v1_ref, v2_ref, mine_ref, got_ref, weight_ref,
    own_ref, give_ref, scale_own, scale_other,
):
    h = pl.program_id(0)
    side = lax.rem(pos_ref[0], 2)
    lane = lax.broadcasted_iota(jnp.int32, (TOK, LANES), 1)

    @pl.when(h == 0)
    def _():
        def scales(here, there):
            (m0, l0), (m1, l1) = here, there
            top = jnp.maximum(m0, m1)
            f0 = jnp.exp2(m0 - top)
            scale = f0 / (l0 * f0 + l1 * jnp.exp2(m1 - top))
            return jnp.transpose(
                jnp.concatenate([scale, jnp.zeros((LANES - HEADS, TOK), F32)], 0)
            )

        at = lambda ref, k: (ref[k * 8 : k * 8 + 8, :], ref[k * 8 + 8 : k * 8 + 16, :])
        scale_own[...] = scales(at(mine_ref, 0), at(got_ref, 2))
        scale_other[...] = scales(at(mine_ref, 2), at(got_ref, 0))
        own_ref[...] = jnp.zeros_like(own_ref)
        give_ref[...] = jnp.zeros_like(give_ref)

    column = lambda ref: jnp.sum(jnp.where(lane == h, ref[...], 0.0), -1, keepdims=True)
    v0, v1, v2 = v0_ref[...], v1_ref[...], v2_ref[...]
    w = lambda n: w_ref[0, :, n * TOK : (n + 1) * TOK]
    mine = dot(w(0), v0) + dot(w(1), v1) + dot(w(2), v2)
    other = dot(w(3), jnp.where(side == 0, v0, v1)) + dot(w(4), jnp.where(side == 0, v1, v2))
    own_ref[...] += dot((mine * column(scale_own)).astype(BF16), weight_ref[...])
    give_ref[...] += dot((other * column(scale_other)).astype(BF16), weight_ref[...])


def run_values(position, weights, v0, v1, v2, mine, got, attend_weight):
    head = pl.BlockSpec((TOK, HD), lambda h, pos: (0, h))
    fixed = lambda shape: pl.BlockSpec(shape, lambda h, pos: (0,) * len(shape))
    return pl.pallas_call(
        values_kernel,
        grid_spec=pltpu.PrefetchScalarGridSpec(
            num_scalar_prefetch=1,
            grid=(HEADS,),
            in_specs=[
                pl.BlockSpec((1, TOK, 5 * TOK), lambda h, pos: (h, 0, 0)),
                head, head, head,
                fixed((4 * HEADS, TOK)),
                fixed((4 * HEADS, TOK)),
                pl.BlockSpec((HD, EMB), lambda h, pos: (h, 0)),
            ],
            out_specs=[fixed((TOK, EMB)), fixed((TOK, EMB))],
            scratch_shapes=[pltpu.VMEM((TOK, LANES), F32)] * 2,
        ),
        out_shape=[jax.ShapeDtypeStruct((TOK, EMB), F32)] * 2,
        cost_estimate=pl.CostEstimate(
            flops=700_000_000, bytes_accessed=8 << 20, transcendentals=1 << 12
        ),
        name="values",
    )(position, weights, v0, v1, v2, mine, got, attend_weight)


def shift(value, steps):
    return lax.ppermute(value, "ctx", [(s, s + steps) for s in range(N_CTX - steps)])


def swap(value):
    return lax.ppermute(value, "ctx", [(s, s ^ 1) for s in range(N_CTX)])


def per_device(
    query_rows, key_rows, value_rows, channels, step_low, step_proj, step_bias, decay_log,
    state_maps, attend_weight, mixer_weight,
):
    position = lax.axis_index("ctx").astype(jnp.int32).reshape(1)
    k1 = shift(key_rows, 2)
    other = swap(query_rows)
    k2 = shift(key_rows, 4)
    v1 = shift(value_rows, 2)
    v2 = shift(value_rows, 4)

    y, cum, send, out_hi, out_lo = run_mixer(
        step_low, step_proj, step_bias, channels, decay_log, state_maps
    )
    got = lax.all_to_all(send, "ctx", 0, 0, tiled=True)
    given = run_prefix(position, got, decay_log)
    enter = lax.all_to_all(given, "ctx", 0, 0, tiled=True)

    weights, stats = run_scores(position, query_rows, other, key_rows, k1, k2)
    got_stats = swap(stats)
    own, give = run_values(position, weights, value_rows, v1, v2, stats, got_stats, attend_weight)
    back = swap(give.astype(BF16))
    return run_finish(y, cum, enter, decay_log, out_hi, out_lo, own, back, mixer_weight)


def solution(mesh):
    rows = P(("dp", "ctx"), None)
    return jax.shard_map(
        per_device,
        mesh=mesh,
        in_specs=(rows, rows, rows, rows, rows, P(), P(), P(), P(None, None, ("dp", "ctx")), P(), P()),
        out_specs=rows,
        check_vma=False,
    )
```

```python
import functools
import math

import jax
import jax.numpy as jnp
from jax import lax
from jax.experimental import pallas as pl
from jax.experimental.pallas import tpu as pltpu
from jax.sharding import PartitionSpec as P


HD = 128
HEADS = 8
TOK = 256
NS = 16
CH = 2048
EMB = 128
CW = 512
LANES = 128
BLK = 16
N_CTX = 64
LOG2E = 1.4426950408889634
SCALE2 = LOG2E / math.sqrt(HD)
VMEM = pl.BlockSpec(memory_space=pltpu.VMEM)
SMEM = pl.BlockSpec(memory_space=pltpu.SMEM)
AWAY = pl.BlockSpec(memory_space=pltpu.HBM)
F32 = jnp.float32
BF16 = jnp.bfloat16


def dot(a, b):
    return jnp.dot(a, b, preferred_element_type=F32)


def dot_t(a, b):
    return lax.dot_general(a, b, (((1,), (1,)), ((), ())), preferred_element_type=F32)


def pieces(x):
    hi = x.astype(BF16)
    rest = x - hi.astype(F32)
    mid = rest.astype(BF16)
    low = (rest - mid.astype(F32)).astype(BF16)
    return hi, mid, low


def softplus(v):
    return jnp.maximum(v, 0.0) + jnp.log1p(jnp.exp(-jnp.abs(v)))


def mixer_kernel(
    low_ref, proj_ref, bias_ref, chan_ref, log_ref, maps_ref,
    y_ref, cum_ref, send_ref, out_ref,
    step_s, flow_s, in_s,
):
    groups = CW // LANES

    @pl.when(pl.program_id(0) == 0)
    def _():
        in_map = maps_ref[0]
        for t in range(TOK):
            in_s[t] = jnp.broadcast_to(in_map[:, t : t + 1], (NS, LANES))
        spread = (
            lax.broadcasted_iota(jnp.int32, (NS, BLK * NS), 1) % NS
            == lax.broadcasted_iota(jnp.int32, (NS, BLK * NS), 0)
        ).astype(F32).astype(BF16)
        keep = (
            lax.broadcasted_iota(jnp.int32, (TOK, BLK * NS), 1) // NS
            == lax.broadcasted_iota(jnp.int32, (TOK, BLK * NS), 0) % BLK
        )
        hi, mid, _ = pieces(jnp.transpose(maps_ref[1]))
        for k, piece in enumerate((hi, mid)):
            rows = jnp.where(keep, dot(piece, spread), 0.0).astype(BF16)
            out_ref[:, k * BLK : (k + 1) * BLK, :] = rows.reshape(TOK // BLK, BLK, BLK * NS)

    rows = 64
    part = rows // BLK
    half = 2 * LANES
    shape = (rows, 2 * rows)
    triangle = (
        lax.broadcasted_iota(jnp.int32, shape, 0)
        >= lax.broadcasted_iota(jnp.int32, shape, 1) % rows
    ).astype(F32).astype(BF16)
    totals = []
    for c in range(CW // half):
        lanes = slice(c * half, (c + 1) * half)
        carry = jnp.zeros((1, half), F32)
        for r in range(TOK // rows):
            at = slice(r * rows, (r + 1) * rows)
            step = softplus(dot(low_ref[at, :], proj_ref[:, lanes]) + bias_ref[:, lanes])
            to = slice(r * part, (r + 1) * part)
            step_s[to, :, lanes] = step.reshape(part, BLK, half)
            flow = step * chan_ref[at, lanes].astype(F32)
            flow_s[to, :, lanes] = flow.reshape(part, BLK, half)
            hi, mid, _ = pieces(step)
            cum = dot(triangle, jnp.concatenate([hi, mid], 0)) + carry
            cum_ref[to, :, lanes] = cum.reshape(part, BLK, half)
            carry = cum[rows - 1 : rows, :]
        totals.append(carry)

    rate = -jnp.exp(log_ref[...]) * LOG2E
    rates = [rate[:, g * LANES : (g + 1) * LANES] for g in range(groups)]

    def block(j, states):
        states = list(states)
        past = []
        for t in range(BLK):
            gain = in_s[j * BLK + t]
            now = []
            for g in range(groups):
                lanes = slice(g * LANES, (g + 1) * LANES)
                decay = jnp.exp2(step_s[j, t : t + 1, lanes] * rates[g])
                states[g] = decay * states[g] + gain * flow_s[j, t : t + 1, lanes]
                now.append(states[g].astype(BF16))
            past.append(jnp.concatenate(now, 1))
        both = dot(out_ref[j], jnp.concatenate(past, 0))
        y_ref[j] = both[:BLK, :] + both[BLK:, :]
        return tuple(states)

    states = lax.fori_loop(
        0, TOK // BLK, block, tuple(jnp.zeros((NS, LANES), F32) for _ in range(groups)), unroll=2
    )
    total = jnp.concatenate(totals, 1)
    hi, mid, low = (v.astype(F32) for v in pieces(total))
    for g in range(groups):
        lanes = slice(g * LANES, (g + 1) * LANES)
        for k in range(NS // 4):
            send_ref[g * 4 + k] = jnp.concatenate(
                [
                    states[g][4 * k : 4 * k + 4, :], hi[:, lanes], mid[:, lanes], low[:, lanes],
                    jnp.zeros((1, LANES), F32),
                ],
                0,
            ).astype(BF16)


def run_mixer(step_low, step_proj, step_bias, channels, decay_log, state_maps):
    blocked = (TOK // BLK, BLK, CW)
    whole = jax.ShapeDtypeStruct((TOK // BLK, BLK, CH), F32)
    out_map = (TOK // BLK, 2 * BLK, BLK * NS)
    fixed = lambda shape: pl.BlockSpec(shape, lambda i: (0,) * len(shape))
    return pl.pallas_call(
        mixer_kernel,
        grid=(CH // CW,),
        in_specs=[
            fixed((TOK, 128)),
            pl.BlockSpec((128, CW), lambda i: (0, i)),
            pl.BlockSpec((1, CW), lambda i: (0, i)),
            pl.BlockSpec((TOK, CW), lambda i: (0, i)),
            pl.BlockSpec((NS, CW), lambda i: (0, i)),
            fixed((2, NS, TOK)),
        ],
        out_specs=[
            pl.BlockSpec(blocked, lambda i: (0, 0, i)),
            pl.BlockSpec(blocked, lambda i: (0, 0, i)),
            pl.BlockSpec((CW // LANES * 4, 8, LANES), lambda i: (i, 0, 0)),
            fixed(out_map),
        ],
        out_shape=[
            whole, whole, jax.ShapeDtypeStruct((N_CTX, 8, LANES), BF16),
            jax.ShapeDtypeStruct(out_map, BF16),
        ],
        scratch_shapes=[
            pltpu.VMEM(blocked, F32),
            pltpu.VMEM(blocked, F32),
            pltpu.VMEM((TOK, NS, LANES), F32),
        ],
        cost_estimate=pl.CostEstimate(
            flops=6_000_000_000, bytes_accessed=8 << 20, transcendentals=8 << 20
        ),
        name="mixer",
    )(step_low, step_proj, step_bias.reshape(1, CH), channels, decay_log, state_maps)


def prefix_kernel(pos_ref, got_ref, log_ref, out_ref):
    part = lax.rem(pos_ref[0], 4)
    rates = -jnp.exp(log_ref[...]) * LOG2E
    rate = rates[0:4]
    for k in range(1, 4):
        rate = jnp.where(part == k, rates[4 * k : 4 * k + 4], rate)
    state = jnp.zeros((4, LANES), F32)
    for s in range(N_CTX):
        out_ref[s] = state
        got = got_ref[s].astype(F32)
        total = got[4:5] + got[5:6] + got[6:7]
        state = jnp.exp2(rate * total) * state + got[0:4]


def run_prefix(position, got, decay_log):
    return pl.pallas_call(
        prefix_kernel,
        grid_spec=pltpu.PrefetchScalarGridSpec(
            num_scalar_prefetch=1,
            grid=(1,),
            in_specs=[
                pl.BlockSpec((N_CTX, 8, LANES), lambda i, pos: (0, 0, 0)),
                pl.BlockSpec((NS, LANES), lambda i, pos: (0, pos[0] // 4)),
            ],
            out_specs=pl.BlockSpec((N_CTX, 4, LANES), lambda i, pos: (0, 0, 0)),
        ),
        out_shape=jax.ShapeDtypeStruct((N_CTX, 4, LANES), F32),
        cost_estimate=pl.CostEstimate(flops=1 << 20, bytes_accessed=1 << 18, transcendentals=1 << 15),
        compiler_params=pltpu.CompilerParams(vmem_limit_bytes=8 << 20),
        name="prefix",
    )(position, got, decay_log)


def enter_kernel(
    y_ref, cum_ref, enter_ref, log_ref, out_ref, weight_ref, o_ref, total_s,
):
    groups = CW // LANES
    i = pl.program_id(0)
    rate = -jnp.exp(log_ref[...]) * LOG2E
    rates = [rate[:, g * LANES : (g + 1) * LANES] for g in range(groups)]
    enter = [
        jnp.concatenate([enter_ref[(i * groups + g) * 4 + k] for k in range(4)], 0)
        for g in range(groups)
    ]

    def block(j, carry):
        past = []
        for t in range(BLK):
            now = []
            for g in range(groups):
                lanes = slice(g * LANES, (g + 1) * LANES)
                decay = jnp.exp2(cum_ref[j, t : t + 1, lanes] * rates[g])
                now.append((decay * enter[g]).astype(BF16))
            past.append(jnp.concatenate(now, 1))
        both = dot(out_ref[j], jnp.concatenate(past, 0))
        rows = pl.ds(pl.multiple_of(j * BLK, BLK), BLK)
        total_s[i, rows, :] = y_ref[j] + both[:BLK, :] + both[BLK:, :]
        return carry

    lax.fori_loop(0, TOK // BLK, block, 0, unroll=2)

    @pl.when(i == CH // CW - 1)
    def _():
        square = jnp.zeros((TOK, LANES), F32)
        for k in range(CH // CW):
            for g in range(groups):
                piece = total_s[k, :, g * LANES : (g + 1) * LANES]
                square += piece * piece
        inverse = lax.rsqrt(jnp.sum(square, -1, keepdims=True) * (1.0 / CH) + 1e-05)
        mixed = jnp.zeros((TOK, EMB), F32)
        for k in range(CH // CW):
            mixed += dot((total_s[k] * inverse).astype(BF16), weight_ref[k * CW : (k + 1) * CW, :])
        o_ref[...] = mixed


def run_enter(y, cum, enter, decay_log, out_map, mixer_weight):
    blocked = pl.BlockSpec((TOK // BLK, BLK, CW), lambda i: (0, 0, i))
    fixed = lambda shape: pl.BlockSpec(shape, lambda i: (0,) * len(shape))
    return pl.pallas_call(
        enter_kernel,
        grid=(CH // CW,),
        in_specs=[
            blocked,
            blocked,
            VMEM,
            pl.BlockSpec((NS, CW), lambda i: (0, i)),
            fixed((TOK // BLK, 2 * BLK, BLK * NS)),
            fixed((CH, EMB)),
        ],
        out_specs=fixed((TOK, EMB)),
        out_shape=jax.ShapeDtypeStruct((TOK, EMB), F32),
        scratch_shapes=[pltpu.VMEM((CH // CW, TOK, CW), F32)],
        cost_estimate=pl.CostEstimate(
            flops=4_000_000_000, bytes_accessed=6 << 20, transcendentals=8 << 20
        ),
        name="enter",
    )(y, cum, enter, decay_log, out_map, mixer_weight)


def final_kernel(mixed_ref, own_ref, back_ref, o_ref):
    combined = mixed_ref[...] + jnp.transpose(own_ref[...] + back_ref[...].astype(F32))
    mean = jnp.mean(combined * combined, -1, keepdims=True)
    o_ref[...] = (combined * lax.rsqrt(mean + 1e-06)).astype(BF16)


def run_final(mixed, own, back):
    return pl.pallas_call(
        final_kernel,
        in_specs=[pl.BlockSpec(memory_space=pltpu.VMEM)] * 3,
        out_specs=pl.BlockSpec(memory_space=pltpu.VMEM),
        out_shape=jax.ShapeDtypeStruct((TOK, EMB), BF16),
        cost_estimate=pl.CostEstimate(flops=1 << 18, bytes_accessed=1 << 18, transcendentals=256),
        compiler_params=pltpu.CompilerParams(vmem_limit_bytes=8 << 20),
        name="final",
    )(mixed, own, back)


def scores_kernel(pos_ref, q_ref, p_ref, k0_ref, k1_ref, k2_ref, away_ref, stat_ref, raw, w_ref, sems):
    def out(h):
        return pltpu.make_async_copy(w_ref.at[h], away_ref.at[h], sems.at[h])

    def head(h, carry):
        scores_head(h, pos_ref, q_ref, p_ref, k0_ref, k1_ref, k2_ref, w_ref, stat_ref, raw)
        out(h).start()
        return carry

    lax.fori_loop(0, HEADS, head, 0)
    for h in range(HEADS):
        out(h).wait()


def scores_head(h, pos_ref, q_ref, p_ref, k0_ref, k1_ref, k2_ref, w_ref, stat_ref, raw):
    span = pl.ds(pl.multiple_of(h * HD, HD), HD)
    side = lax.rem(pos_ref[0], 2)
    pair = pos_ref[0] // 2
    gone1 = jnp.where(pair >= 1, 0.0, -1e30).astype(F32)
    gone2 = jnp.where(pair >= 2, 0.0, -1e30).astype(F32)
    key = lax.broadcasted_iota(jnp.int32, (HD, HD), 0)
    asker = lax.broadcasted_iota(jnp.int32, (HD, HD), 1)
    line = lax.broadcasted_iota(jnp.int32, (4 * HEADS, TOK), 0)
    k0, k1, k2 = k0_ref[:, span], k1_ref[:, span], k2_ref[:, span]
    zero = jnp.zeros((HD, HD), BF16)

    def weigh(first, kinds, gone, slot):
        tops, sums = [], []
        for side_q in range(2):
            lanes = slice(side_q * HD, (side_q + 1) * HD)

            def load(n, side_k):
                at = (first + n) * TOK + side_k * HD
                x = raw[at : at + HD, lanes]
                kind = kinds[n][side_k][side_q]
                if kind == "upto":
                    x = jnp.where(key <= asker, x, -1e30)
                if kind == "after":
                    x = jnp.where(key > asker, x, -1e30)
                return x

            top = None
            for n in range(len(kinds)):
                block = None
                for side_k in range(2):
                    if kinds[n][side_k][side_q] != "none":
                        x = jnp.max(load(n, side_k), 0, keepdims=True)
                        block = x if block is None else jnp.maximum(block, x)
                block = block * SCALE2 + gone[n]
                top = block if top is None else jnp.maximum(top, block)
            total = jnp.zeros((1, HD), F32)
            for n in range(len(kinds)):
                level = top - gone[n]
                for side_k in range(2):
                    at = (first + n) * TOK + side_k * HD
                    if kinds[n][side_k][side_q] == "none":
                        w_ref[h, at : at + HD, lanes] = zero
                        continue
                    terms = jnp.exp2(load(n, side_k) * SCALE2 - level)
                    total += jnp.sum(terms, 0, keepdims=True)
                    w_ref[h, at : at + HD, lanes] = terms.astype(BF16)
            tops.append(top)
            sums.append(total)
        now = jnp.where(line == slot + h, jnp.concatenate(tops, 1), stat_ref[...])
        stat_ref[...] = jnp.where(line == slot + HEADS + h, jnp.concatenate(sums, 1), now)

    q, other = q_ref[:, span], p_ref[:, span]
    for n, k in enumerate((k0, k1, k2)):
        raw[n * TOK : (n + 1) * TOK, :] = dot_t(k, q)
    raw[3 * TOK : 4 * TOK, :] = dot_t(jnp.where(side == 0, k0, k1), other)
    raw[4 * TOK : 5 * TOK, :] = dot_t(jnp.where(side == 0, k1, k2), other)
    every = (("all", "all"), ("all", "all"))
    weigh(
        0,
        ((("upto", "all"), ("none", "upto")), every, (("after", "none"), ("all", "after"))),
        (jnp.float32(0.0), gone1, gone2),
        0,
    )
    weigh(
        3,
        (every, every),
        (jnp.where(side == 0, 0.0, gone1), jnp.where(side == 0, gone1, gone2)),
        2 * HEADS,
    )


def run_scores(position, query, other, k0, k1, k2):
    return pl.pallas_call(
        scores_kernel,
        in_specs=[SMEM] + [VMEM] * 5,
        out_specs=[AWAY, VMEM],
        scratch_shapes=[
            pltpu.VMEM((5 * TOK, TOK), F32),
            pltpu.VMEM((HEADS, 5 * TOK, TOK), BF16),
            pltpu.SemaphoreType.DMA((HEADS,)),
        ],
        out_shape=[
            pltpu.HBM((HEADS, 5 * TOK, TOK), BF16),
            jax.ShapeDtypeStruct((4 * HEADS, TOK), F32),
        ],
        compiler_params=pltpu.CompilerParams(vmem_limit_bytes=16 << 20),
        cost_estimate=pl.CostEstimate(
            flops=700_000_000, bytes_accessed=8 << 20, transcendentals=3 << 20
        ),
        name="scores",
    )(position, query, other, k0, k1, k2)


def dot_0(a, b):
    return lax.dot_general(a, b, (((0,), (0,)), ((), ())), preferred_element_type=F32)


def values_kernel(
    mine, pos_ref, away_ref, v0_ref, v1_ref, v2_ref, stat_ref, got_ref, weight_ref, o_ref,
    scale_s, sum_s, w_ref, sems,
):
    rows = (0, 3 * TOK) if mine else (3 * TOK, 2 * TOK)

    def fetch(h):
        return pltpu.make_async_copy(away_ref.at[h, pl.ds(*rows), :], w_ref.at[h], sems.at[h])

    for h in range(HEADS):
        fetch(h).start()
    side = lax.rem(pos_ref[0], 2)
    at = lambda ref, k: (ref[k * 8 : k * 8 + 8, :], ref[k * 8 + 8 : k * 8 + 16, :])
    (m0, l0), (m1, l1) = at(stat_ref, 0 if mine else 2), at(got_ref, 2 if mine else 0)
    top = jnp.maximum(m0, m1)
    f0 = jnp.exp2(m0 - top)
    scale_s[...] = f0 / (l0 * f0 + l1 * jnp.exp2(m1 - top))
    sum_s[...] = jnp.zeros_like(sum_s)
    line = lax.broadcasted_iota(jnp.int32, (HEADS, TOK), 0)

    def head(h, carry):
        span = pl.ds(pl.multiple_of(h * HD, HD), HD)
        scale = jnp.sum(jnp.where(line == h, scale_s[...], 0.0), 0, keepdims=True)
        v0, v1, v2 = v0_ref[:, span], v1_ref[:, span], v2_ref[:, span]
        fetch(h).wait()
        w = lambda n: w_ref[h, n * TOK : (n + 1) * TOK, :]
        if mine:
            taken = dot_0(v0, w(0)) + dot_0(v1, w(1)) + dot_0(v2, w(2))
        else:
            taken = dot_0(jnp.where(side == 0, v0, v1), w(0))
            taken += dot_0(jnp.where(side == 0, v1, v2), w(1))
        sum_s[...] += dot_0(weight_ref[span, :], (taken * scale).astype(BF16))
        return carry

    lax.fori_loop(0, HEADS, head, 0, unroll=2)
    o_ref[...] = sum_s[...].astype(o_ref.dtype)


def run_values(mine, position, weights, v0, v1, v2, stats, got, attend_weight):
    return pl.pallas_call(
        functools.partial(values_kernel, mine),
        in_specs=[SMEM, AWAY] + [VMEM] * 6,
        out_specs=VMEM,
        scratch_shapes=[
            pltpu.VMEM((HEADS, TOK), F32),
            pltpu.VMEM((EMB, TOK), F32),
            pltpu.VMEM((HEADS, (3 if mine else 2) * TOK, TOK), BF16),
            pltpu.SemaphoreType.DMA((HEADS,)),
        ],
        out_shape=jax.ShapeDtypeStruct((EMB, TOK), F32 if mine else BF16),
        compiler_params=pltpu.CompilerParams(vmem_limit_bytes=16 << 20),
        cost_estimate=pl.CostEstimate(
            flops=400_000_000, bytes_accessed=4 << 20, transcendentals=1 << 12
        ),
        name="values_own" if mine else "values_other",
    )(position, weights, v0, v1, v2, stats, got, attend_weight)


def shift(value, steps):
    return lax.ppermute(value, "ctx", [(s, s + steps) for s in range(N_CTX - steps)])


def swap(value):
    return lax.ppermute(value, "ctx", [(s, s ^ 1) for s in range(N_CTX)])


def per_device(
    query_rows, key_rows, value_rows, channels, step_low, step_proj, step_bias, decay_log,
    state_maps, attend_weight, mixer_weight,
):
    position = lax.axis_index("ctx").astype(jnp.int32).reshape(1)
    other = swap(query_rows)
    k1 = shift(key_rows, 2)
    k2 = shift(key_rows, 4)
    y, cum, send, out_map = run_mixer(
        step_low, step_proj, step_bias, channels, decay_log, state_maps
    )
    got = lax.all_to_all(send, "ctx", 0, 0, tiled=True)
    v1 = shift(value_rows, 2)
    v2 = shift(value_rows, 4)
    weights, stats = run_scores(position, query_rows, other, key_rows, k1, k2)
    given = run_prefix(position, got, decay_log)
    enter = lax.all_to_all(given, "ctx", 0, 0, tiled=True)
    got_stats = swap(stats)
    blocks = (value_rows, v1, v2, stats, got_stats, attend_weight)
    weights = pltpu.with_memory_space_constraint(weights, pltpu.HBM)
    give = run_values(False, position, weights, *blocks)
    back = swap(give)
    mixed = run_enter(y, cum, enter, decay_log, out_map, mixer_weight)
    own = run_values(True, position, weights, *blocks)
    return run_final(mixed, own, back)


def solution(mesh):
    rows = P(("dp", "ctx"), None)
    return jax.shard_map(
        per_device,
        mesh=mesh,
        in_specs=(rows, rows, rows, rows, rows, P(), P(), P(), P(None, None, ("dp", "ctx")), P(), P()),
        out_specs=rows,
        check_vma=False,
    )
```

```python
import functools
import math

import jax
import jax.numpy as jnp
from jax import lax
from jax.experimental import pallas as pl
from jax.experimental.pallas import tpu as pltpu
from jax.sharding import PartitionSpec as P


HD = 128
HEADS = 8
TOK = 256
NS = 16
CH = 2048
EMB = 128
CW = 512
LANES = 128
BLK = 16
N_CTX = 64
LOG2E = 1.4426950408889634
SCALE2 = LOG2E / math.sqrt(HD)
VMEM = pl.BlockSpec(memory_space=pltpu.VMEM)
SMEM = pl.BlockSpec(memory_space=pltpu.SMEM)
AWAY = pl.BlockSpec(memory_space=pltpu.HBM)
F32 = jnp.float32
BF16 = jnp.bfloat16


def dot(a, b):
    return jnp.dot(a, b, preferred_element_type=F32)


def dot_t(a, b):
    return lax.dot_general(a, b, (((1,), (1,)), ((), ())), preferred_element_type=F32)


def pieces(x):
    hi = x.astype(BF16)
    rest = x - hi.astype(F32)
    mid = rest.astype(BF16)
    low = (rest - mid.astype(F32)).astype(BF16)
    return hi, mid, low


def softplus(v):
    return jnp.maximum(v, 0.0) + jnp.log1p(jnp.exp(-jnp.abs(v)))


def mixer_kernel(
    low_ref, proj_ref, bias_ref, chan_ref, log_ref, maps_ref,
    y_ref, cum_ref, send_ref, out_ref,
    step_s, flow_s, in_s,
):
    groups = CW // LANES

    @pl.when(pl.program_id(0) == 0)
    def _():
        in_map = maps_ref[0]
        for t in range(TOK):
            in_s[t] = jnp.broadcast_to(in_map[:, t : t + 1], (NS, LANES))
        spread = (
            lax.broadcasted_iota(jnp.int32, (NS, BLK * NS), 1) % NS
            == lax.broadcasted_iota(jnp.int32, (NS, BLK * NS), 0)
        ).astype(F32).astype(BF16)
        keep = (
            lax.broadcasted_iota(jnp.int32, (TOK, BLK * NS), 1) // NS
            == lax.broadcasted_iota(jnp.int32, (TOK, BLK * NS), 0) % BLK
        )
        hi, mid, _ = pieces(jnp.transpose(maps_ref[1]))
        for k, piece in enumerate((hi, mid)):
            rows = jnp.where(keep, dot(piece, spread), 0.0).astype(BF16)
            out_ref[:, k * BLK : (k + 1) * BLK, :] = rows.reshape(TOK // BLK, BLK, BLK * NS)

    rows = 64
    part = rows // BLK
    half = 2 * LANES
    shape = (rows, 2 * rows)
    triangle = (
        lax.broadcasted_iota(jnp.int32, shape, 0)
        >= lax.broadcasted_iota(jnp.int32, shape, 1) % rows
    ).astype(F32).astype(BF16)
    totals = []
    for c in range(CW // half):
        lanes = slice(c * half, (c + 1) * half)
        carry = jnp.zeros((1, half), F32)
        for r in range(TOK // rows):
            at = slice(r * rows, (r + 1) * rows)
            step = softplus(dot(low_ref[at, :], proj_ref[:, lanes]) + bias_ref[:, lanes])
            to = slice(r * part, (r + 1) * part)
            step_s[to, :, lanes] = step.reshape(part, BLK, half)
            flow = step * chan_ref[at, lanes].astype(F32)
            flow_s[to, :, lanes] = flow.reshape(part, BLK, half)
            hi, mid, _ = pieces(step)
            cum = dot(triangle, jnp.concatenate([hi, mid], 0)) + carry
            cum_ref[to, :, lanes] = cum.reshape(part, BLK, half)
            carry = cum[rows - 1 : rows, :]
        totals.append(carry)

    rate = -jnp.exp(log_ref[...]) * LOG2E
    rates = [rate[:, g * LANES : (g + 1) * LANES] for g in range(groups)]

    def block(j, states):
        states = list(states)
        past = []
        for t in range(BLK):
            gain = in_s[j * BLK + t]
            now = []
            for g in range(groups):
                lanes = slice(g * LANES, (g + 1) * LANES)
                decay = jnp.exp2(step_s[j, t : t + 1, lanes] * rates[g])
                states[g] = decay * states[g] + gain * flow_s[j, t : t + 1, lanes]
                now.append(states[g].astype(BF16))
            past.append(jnp.concatenate(now, 1))
        both = dot(out_ref[j], jnp.concatenate(past, 0))
        y_ref[j] = both[:BLK, :] + both[BLK:, :]
        return tuple(states)

    states = lax.fori_loop(
        0, TOK // BLK, block, tuple(jnp.zeros((NS, LANES), F32) for _ in range(groups)), unroll=4
    )
    total = jnp.concatenate(totals, 1)
    hi, mid, low = (v.astype(F32) for v in pieces(total))
    for g in range(groups):
        lanes = slice(g * LANES, (g + 1) * LANES)
        for k in range(NS // 4):
            send_ref[g * 4 + k] = jnp.concatenate(
                [
                    states[g][4 * k : 4 * k + 4, :], hi[:, lanes], mid[:, lanes], low[:, lanes],
                    jnp.zeros((1, LANES), F32),
                ],
                0,
            ).astype(BF16)


def run_mixer(step_low, step_proj, step_bias, channels, decay_log, state_maps):
    blocked = (TOK // BLK, BLK, CW)
    whole = jax.ShapeDtypeStruct((TOK // BLK, BLK, CH), F32)
    out_map = (TOK // BLK, 2 * BLK, BLK * NS)
    fixed = lambda shape: pl.BlockSpec(shape, lambda i: (0,) * len(shape))
    return pl.pallas_call(
        mixer_kernel,
        grid=(CH // CW,),
        in_specs=[
            fixed((TOK, 128)),
            pl.BlockSpec((128, CW), lambda i: (0, i)),
            pl.BlockSpec((1, CW), lambda i: (0, i)),
            pl.BlockSpec((TOK, CW), lambda i: (0, i)),
            pl.BlockSpec((NS, CW), lambda i: (0, i)),
            fixed((2, NS, TOK)),
        ],
        out_specs=[
            pl.BlockSpec(blocked, lambda i: (0, 0, i)),
            pl.BlockSpec(blocked, lambda i: (0, 0, i)),
            pl.BlockSpec((CW // LANES * 4, 8, LANES), lambda i: (i, 0, 0)),
            fixed(out_map),
        ],
        out_shape=[
            whole, whole, jax.ShapeDtypeStruct((N_CTX, 8, LANES), BF16),
            jax.ShapeDtypeStruct(out_map, BF16),
        ],
        scratch_shapes=[
            pltpu.VMEM(blocked, F32),
            pltpu.VMEM(blocked, F32),
            pltpu.VMEM((TOK, NS, LANES), F32),
        ],
        cost_estimate=pl.CostEstimate(
            flops=6_000_000_000, bytes_accessed=8 << 20, transcendentals=8 << 20
        ),
        name="mixer",
    )(step_low, step_proj, step_bias.reshape(1, CH), channels, decay_log, state_maps)


def prefix_kernel(pos_ref, got_ref, log_ref, out_ref):
    part = lax.rem(pos_ref[0], 4)
    rates = -jnp.exp(log_ref[...]) * LOG2E
    rate = rates[0:4]
    for k in range(1, 4):
        rate = jnp.where(part == k, rates[4 * k : 4 * k + 4], rate)
    state = jnp.zeros((4, LANES), F32)
    for s in range(N_CTX):
        out_ref[s] = state
        got = got_ref[s].astype(F32)
        total = got[4:5] + got[5:6] + got[6:7]
        state = jnp.exp2(rate * total) * state + got[0:4]


def run_prefix(position, got, decay_log):
    return pl.pallas_call(
        prefix_kernel,
        grid_spec=pltpu.PrefetchScalarGridSpec(
            num_scalar_prefetch=1,
            grid=(1,),
            in_specs=[
                pl.BlockSpec((N_CTX, 8, LANES), lambda i, pos: (0, 0, 0)),
                pl.BlockSpec((NS, LANES), lambda i, pos: (0, pos[0] // 4)),
            ],
            out_specs=pl.BlockSpec((N_CTX, 4, LANES), lambda i, pos: (0, 0, 0)),
        ),
        out_shape=jax.ShapeDtypeStruct((N_CTX, 4, LANES), F32),
        cost_estimate=pl.CostEstimate(flops=1 << 20, bytes_accessed=1 << 18, transcendentals=1 << 15),
        compiler_params=pltpu.CompilerParams(vmem_limit_bytes=8 << 20),
        name="prefix",
    )(position, got, decay_log)


def enter_kernel(
    y_ref, cum_ref, enter_ref, log_ref, out_ref, weight_ref, own_ref, back_ref, o_ref, total_s,
):
    groups = CW // LANES
    i = pl.program_id(0)
    rate = -jnp.exp(log_ref[...]) * LOG2E
    rates = [rate[:, g * LANES : (g + 1) * LANES] for g in range(groups)]
    enter = [
        jnp.concatenate([enter_ref[(i * groups + g) * 4 + k] for k in range(4)], 0)
        for g in range(groups)
    ]

    def block(j, carry):
        past = []
        for t in range(BLK):
            now = []
            for g in range(groups):
                lanes = slice(g * LANES, (g + 1) * LANES)
                decay = jnp.exp2(cum_ref[j, t : t + 1, lanes] * rates[g])
                now.append((decay * enter[g]).astype(BF16))
            past.append(jnp.concatenate(now, 1))
        both = dot(out_ref[j], jnp.concatenate(past, 0))
        rows = pl.ds(pl.multiple_of(j * BLK, BLK), BLK)
        total_s[i, rows, :] = y_ref[j] + both[:BLK, :] + both[BLK:, :]
        return carry

    lax.fori_loop(0, TOK // BLK, block, 0, unroll=4)

    @pl.when(i == CH // CW - 1)
    def _():
        square = jnp.zeros((TOK, LANES), F32)
        for k in range(CH // CW):
            for g in range(groups):
                piece = total_s[k, :, g * LANES : (g + 1) * LANES]
                square += piece * piece
        inverse = lax.rsqrt(jnp.sum(square, -1, keepdims=True) * (1.0 / CH) + 1e-05)
        combined = jnp.transpose(own_ref[...] + back_ref[...].astype(F32))
        for k in range(CH // CW):
            combined += dot((total_s[k] * inverse).astype(BF16), weight_ref[k * CW : (k + 1) * CW, :])
        mean = jnp.mean(combined * combined, -1, keepdims=True)
        o_ref[...] = (combined * lax.rsqrt(mean + 1e-06)).astype(BF16)


def run_enter(y, cum, enter, decay_log, out_map, mixer_weight, own, back):
    blocked = pl.BlockSpec((TOK // BLK, BLK, CW), lambda i: (0, 0, i))
    far = lambda x: pltpu.with_memory_space_constraint(x, pltpu.HBM)
    fixed = lambda shape: pl.BlockSpec(shape, lambda i: (0,) * len(shape))
    return pl.pallas_call(
        enter_kernel,
        grid=(CH // CW,),
        in_specs=[
            blocked,
            blocked,
            VMEM,
            pl.BlockSpec((NS, CW), lambda i: (0, i)),
            fixed((TOK // BLK, 2 * BLK, BLK * NS)),
            fixed((CH, EMB)),
            VMEM,
            VMEM,
        ],
        out_specs=fixed((TOK, EMB)),
        out_shape=jax.ShapeDtypeStruct((TOK, EMB), BF16),
        scratch_shapes=[pltpu.VMEM((CH // CW, TOK, CW), F32)],
        cost_estimate=pl.CostEstimate(
            flops=4_000_000_000, bytes_accessed=6 << 20, transcendentals=8 << 20
        ),
        compiler_params=pltpu.CompilerParams(vmem_limit_bytes=20 << 20),
        name="enter",
    )(far(y), far(cum), enter, far(decay_log), far(out_map), far(mixer_weight), own, back)


def scores_kernel(pos_ref, q_ref, p_ref, k0_ref, k1_ref, k2_ref, away_ref, stat_ref, raw, w_ref, sems):
    def out(h):
        return pltpu.make_async_copy(w_ref.at[h], away_ref.at[h], sems.at[h])

    def head(h, carry):
        scores_head(h, pos_ref, q_ref, p_ref, k0_ref, k1_ref, k2_ref, w_ref, stat_ref, raw)
        out(h).start()
        return carry

    lax.fori_loop(0, HEADS, head, 0)
    for h in range(HEADS):
        out(h).wait()


def scores_head(h, pos_ref, q_ref, p_ref, k0_ref, k1_ref, k2_ref, w_ref, stat_ref, raw):
    span = pl.ds(pl.multiple_of(h * HD, HD), HD)
    side = lax.rem(pos_ref[0], 2)
    pair = pos_ref[0] // 2
    gone1 = jnp.where(pair >= 1, 0.0, -1e30).astype(F32)
    gone2 = jnp.where(pair >= 2, 0.0, -1e30).astype(F32)
    key = lax.broadcasted_iota(jnp.int32, (HD, HD), 0)
    asker = lax.broadcasted_iota(jnp.int32, (HD, HD), 1)
    line = lax.broadcasted_iota(jnp.int32, (4 * HEADS, TOK), 0)
    k0, k1, k2 = k0_ref[:, span], k1_ref[:, span], k2_ref[:, span]
    zero = jnp.zeros((HD, HD), BF16)

    def weigh(first, kinds, gone, slot):
        tops, sums = [], []
        for side_q in range(2):
            lanes = slice(side_q * HD, (side_q + 1) * HD)

            def load(n, side_k):
                at = (first + n) * TOK + side_k * HD
                x = raw[at : at + HD, lanes]
                kind = kinds[n][side_k][side_q]
                if kind == "upto":
                    x = jnp.where(key <= asker, x, -1e30)
                if kind == "after":
                    x = jnp.where(key > asker, x, -1e30)
                return x

            top = None
            for n in range(len(kinds)):
                block = None
                for side_k in range(2):
                    if kinds[n][side_k][side_q] != "none":
                        x = jnp.max(load(n, side_k), 0, keepdims=True)
                        block = x if block is None else jnp.maximum(block, x)
                block = block * SCALE2 + gone[n]
                top = block if top is None else jnp.maximum(top, block)
            total = jnp.zeros((1, HD), F32)
            for n in range(len(kinds)):
                level = top - gone[n]
                for side_k in range(2):
                    at = (first + n) * TOK + side_k * HD
                    if kinds[n][side_k][side_q] == "none":
                        w_ref[h, at : at + HD, lanes] = zero
                        continue
                    terms = jnp.exp2(load(n, side_k) * SCALE2 - level)
                    total += jnp.sum(terms, 0, keepdims=True)
                    w_ref[h, at : at + HD, lanes] = terms.astype(BF16)
            tops.append(top)
            sums.append(total)
        now = jnp.where(line == slot + h, jnp.concatenate(tops, 1), stat_ref[...])
        stat_ref[...] = jnp.where(line == slot + HEADS + h, jnp.concatenate(sums, 1), now)

    q, other = q_ref[:, span], p_ref[:, span]
    for n, k in enumerate((k0, k1, k2)):
        raw[n * TOK : (n + 1) * TOK, :] = dot_t(k, q)
    raw[3 * TOK : 4 * TOK, :] = dot_t(jnp.where(side == 0, k0, k1), other)
    raw[4 * TOK : 5 * TOK, :] = dot_t(jnp.where(side == 0, k1, k2), other)
    every = (("all", "all"), ("all", "all"))
    weigh(
        0,
        ((("upto", "all"), ("none", "upto")), every, (("after", "none"), ("all", "after"))),
        (jnp.float32(0.0), gone1, gone2),
        0,
    )
    weigh(
        3,
        (every, every),
        (jnp.where(side == 0, 0.0, gone1), jnp.where(side == 0, gone1, gone2)),
        2 * HEADS,
    )


def run_scores(position, query, other, k0, k1, k2):
    return pl.pallas_call(
        scores_kernel,
        in_specs=[SMEM] + [VMEM] * 5,
        out_specs=[AWAY, VMEM],
        scratch_shapes=[
            pltpu.VMEM((5 * TOK, TOK), F32),
            pltpu.VMEM((HEADS, 5 * TOK, TOK), BF16),
            pltpu.SemaphoreType.DMA((HEADS,)),
        ],
        out_shape=[
            pltpu.HBM((HEADS, 5 * TOK, TOK), BF16),
            jax.ShapeDtypeStruct((4 * HEADS, TOK), F32),
        ],
        compiler_params=pltpu.CompilerParams(vmem_limit_bytes=16 << 20),
        cost_estimate=pl.CostEstimate(
            flops=700_000_000, bytes_accessed=8 << 20, transcendentals=3 << 20
        ),
        name="scores",
    )(position, query, other, k0, k1, k2)


def dot_0(a, b):
    return lax.dot_general(a, b, (((0,), (0,)), ((), ())), preferred_element_type=F32)


def values_kernel(
    mine, pos_ref, away_ref, v0_ref, v1_ref, v2_ref, stat_ref, got_ref, weight_ref, o_ref,
    scale_s, sum_s, w_ref, sems,
):
    rows = (0, 3 * TOK) if mine else (3 * TOK, 2 * TOK)

    def fetch(h):
        return pltpu.make_async_copy(away_ref.at[h, pl.ds(*rows), :], w_ref.at[h], sems.at[h])

    ahead = 3
    for h in range(ahead):
        fetch(h).start()
    side = lax.rem(pos_ref[0], 2)
    at = lambda ref, k: (ref[k * 8 : k * 8 + 8, :], ref[k * 8 + 8 : k * 8 + 16, :])
    (m0, l0), (m1, l1) = at(stat_ref, 0 if mine else 2), at(got_ref, 2 if mine else 0)
    top = jnp.maximum(m0, m1)
    f0 = jnp.exp2(m0 - top)
    scale_s[...] = f0 / (l0 * f0 + l1 * jnp.exp2(m1 - top))
    sum_s[...] = jnp.zeros_like(sum_s)
    line = lax.broadcasted_iota(jnp.int32, (HEADS, TOK), 0)

    def head(h, carry):
        span = pl.ds(pl.multiple_of(h * HD, HD), HD)
        scale = jnp.sum(jnp.where(line == h, scale_s[...], 0.0), 0, keepdims=True)
        v0, v1, v2 = v0_ref[:, span], v1_ref[:, span], v2_ref[:, span]
        fetch(h).wait()

        @pl.when(h + ahead < HEADS)
        def _():
            fetch(h + ahead).start()

        w = lambda n: w_ref[h, n * TOK : (n + 1) * TOK, :]
        if mine:
            taken = dot_0(v0, w(0)) + dot_0(v1, w(1)) + dot_0(v2, w(2))
        else:
            taken = dot_0(jnp.where(side == 0, v0, v1), w(0))
            taken += dot_0(jnp.where(side == 0, v1, v2), w(1))
        sum_s[...] += dot_0(weight_ref[span, :], (taken * scale).astype(BF16))
        return carry

    lax.fori_loop(0, HEADS, head, 0)
    o_ref[...] = sum_s[...].astype(o_ref.dtype)


def run_values(mine, position, weights, v0, v1, v2, stats, got, attend_weight):
    return pl.pallas_call(
        functools.partial(values_kernel, mine),
        in_specs=[SMEM, AWAY] + [VMEM] * 6,
        out_specs=VMEM,
        scratch_shapes=[
            pltpu.VMEM((HEADS, TOK), F32),
            pltpu.VMEM((EMB, TOK), F32),
            pltpu.VMEM((HEADS, (3 if mine else 2) * TOK, TOK), BF16),
            pltpu.SemaphoreType.DMA((HEADS,)),
        ],
        out_shape=jax.ShapeDtypeStruct((EMB, TOK), F32 if mine else BF16),
        compiler_params=pltpu.CompilerParams(vmem_limit_bytes=16 << 20),
        cost_estimate=pl.CostEstimate(
            flops=400_000_000, bytes_accessed=4 << 20, transcendentals=1 << 12
        ),
        name="values_own" if mine else "values_other",
    )(position, weights, v0, v1, v2, stats, got, attend_weight)


def shift(value, steps):
    return lax.ppermute(value, "ctx", [(s, s + steps) for s in range(N_CTX - steps)])


def swap(value):
    return lax.ppermute(value, "ctx", [(s, s ^ 1) for s in range(N_CTX)])


def per_device(
    query_rows, key_rows, value_rows, channels, step_low, step_proj, step_bias, decay_log,
    state_maps, attend_weight, mixer_weight,
):
    position = lax.axis_index("ctx").astype(jnp.int32).reshape(1)
    other = swap(query_rows)
    k1 = shift(key_rows, 2)
    k2 = shift(key_rows, 4)
    v1 = shift(value_rows, 2)
    y, cum, send, out_map = run_mixer(
        step_low, step_proj, step_bias, channels, decay_log, state_maps
    )
    got = lax.all_to_all(send, "ctx", 0, 0, tiled=True)
    v2 = shift(value_rows, 4)
    weights, stats = run_scores(position, query_rows, other, key_rows, k1, k2)
    given = run_prefix(position, got, decay_log)
    enter = lax.all_to_all(given, "ctx", 0, 0, tiled=True)
    got_stats = swap(stats)
    blocks = (value_rows, v1, v2, stats, got_stats, attend_weight)
    weights = pltpu.with_memory_space_constraint(weights, pltpu.HBM)
    give = run_values(False, position, weights, *blocks)
    back = swap(give)
    own = run_values(True, position, weights, *blocks)
    return run_enter(y, cum, enter, decay_log, out_map, mixer_weight, own, back)


def solution(mesh):
    rows = P(("dp", "ctx"), None)
    return jax.shard_map(
        per_device,
        mesh=mesh,
        in_specs=(rows, rows, rows, rows, rows, P(), P(), P(), P(None, None, ("dp", "ctx")), P(), P()),
        out_specs=rows,
        check_vma=False,
    )
```

```python
import functools
import math

import jax
import jax.numpy as jnp
from jax import lax
from jax.experimental import pallas as pl
from jax.experimental.pallas import tpu as pltpu
from jax.sharding import PartitionSpec as P


HD = 128
HEADS = 8
TOK = 256
NS = 16
CH = 2048
EMB = 128
CW = 512
LANES = 128
BLK = 16
N_CTX = 64
LOG2E = 1.4426950408889634
SCALE2 = LOG2E / math.sqrt(HD)
VMEM = pl.BlockSpec(memory_space=pltpu.VMEM)
SMEM = pl.BlockSpec(memory_space=pltpu.SMEM)
AWAY = pl.BlockSpec(memory_space=pltpu.HBM)
F32 = jnp.float32
BF16 = jnp.bfloat16


def dot(a, b):
    return jnp.dot(a, b, preferred_element_type=F32)


def dot_t(a, b):
    return lax.dot_general(a, b, (((1,), (1,)), ((), ())), preferred_element_type=F32)


def pieces(x):
    hi = x.astype(BF16)
    rest = x - hi.astype(F32)
    mid = rest.astype(BF16)
    low = (rest - mid.astype(F32)).astype(BF16)
    return hi, mid, low


def softplus(v):
    return jnp.maximum(v, 0.0) + jnp.log1p(jnp.exp(-jnp.abs(v)))


def mixer_first_kernel(pos_ref, *refs):
    @pl.when(lax.rem(pos_ref[0], 2) == 0)
    def _():
        mixer_tables(*refs)
        mixer_chunk(*refs)


def mixer_rest_kernel(pos_ref, *refs):
    refs = refs[:6] + refs[9:]

    @pl.when(pl.program_id(0) == 0)
    def _():
        mixer_tables(*refs)

    @pl.when((pl.program_id(0) > 0) | (lax.rem(pos_ref[0], 2) == 1))
    def _():
        mixer_chunk(*refs)


def mixer_tables(
    low_ref, proj_ref, bias_ref, chan_ref, log_ref, maps_ref,
    y_ref, cum_ref, send_ref, out_ref,
    step_s, flow_s, in_s,
):
    in_map = maps_ref[0]
    for t in range(TOK):
        in_s[t] = jnp.broadcast_to(in_map[:, t : t + 1], (NS, LANES))
    spread = (
        lax.broadcasted_iota(jnp.int32, (NS, BLK * NS), 1) % NS
        == lax.broadcasted_iota(jnp.int32, (NS, BLK * NS), 0)
    ).astype(F32).astype(BF16)
    keep = (
        lax.broadcasted_iota(jnp.int32, (TOK, BLK * NS), 1) // NS
        == lax.broadcasted_iota(jnp.int32, (TOK, BLK * NS), 0) % BLK
    )
    hi, mid, _ = pieces(jnp.transpose(maps_ref[1]))
    for k, piece in enumerate((hi, mid)):
        rows = jnp.where(keep, dot(piece, spread), 0.0).astype(BF16)
        out_ref[:, k * BLK : (k + 1) * BLK, :] = rows.reshape(TOK // BLK, BLK, BLK * NS)


def mixer_chunk(
    low_ref, proj_ref, bias_ref, chan_ref, log_ref, maps_ref,
    y_ref, cum_ref, send_ref, out_ref,
    step_s, flow_s, in_s,
):
    groups = CW // LANES
    rows = 64
    part = rows // BLK
    half = 2 * LANES
    shape = (rows, 2 * rows)
    triangle = (
        lax.broadcasted_iota(jnp.int32, shape, 0)
        >= lax.broadcasted_iota(jnp.int32, shape, 1) % rows
    ).astype(F32).astype(BF16)
    totals = []
    for c in range(CW // half):
        lanes = slice(c * half, (c + 1) * half)
        carry = jnp.zeros((1, half), F32)
        for r in range(TOK // rows):
            at = slice(r * rows, (r + 1) * rows)
            step = softplus(dot(low_ref[at, :], proj_ref[:, lanes]) + bias_ref[:, lanes])
            to = slice(r * part, (r + 1) * part)
            step_s[to, :, lanes] = step.reshape(part, BLK, half)
            flow = step * chan_ref[at, lanes].astype(F32)
            flow_s[to, :, lanes] = flow.reshape(part, BLK, half)
            hi, mid, _ = pieces(step)
            cum = dot(triangle, jnp.concatenate([hi, mid], 0)) + carry
            cum_ref[to, :, lanes] = cum.reshape(part, BLK, half)
            carry = cum[rows - 1 : rows, :]
        totals.append(carry)

    rate = -jnp.exp(log_ref[...]) * LOG2E
    rates = [rate[:, g * LANES : (g + 1) * LANES] for g in range(groups)]

    def block(j, states):
        states = list(states)
        past = []
        for t in range(BLK):
            gain = in_s[j * BLK + t]
            now = []
            for g in range(groups):
                lanes = slice(g * LANES, (g + 1) * LANES)
                decay = jnp.exp2(step_s[j, t : t + 1, lanes] * rates[g])
                states[g] = decay * states[g] + gain * flow_s[j, t : t + 1, lanes]
                now.append(states[g].astype(BF16))
            past.append(jnp.concatenate(now, 1))
        both = dot(out_ref[j], jnp.concatenate(past, 0))
        y_ref[j] = both[:BLK, :] + both[BLK:, :]
        return tuple(states)

    states = lax.fori_loop(
        0, TOK // BLK, block, tuple(jnp.zeros((NS, LANES), F32) for _ in range(groups)), unroll=4
    )
    total = jnp.concatenate(totals, 1)
    hi, mid, low = (v.astype(F32) for v in pieces(total))
    for g in range(groups):
        lanes = slice(g * LANES, (g + 1) * LANES)
        for k in range(NS // 4):
            send_ref[g * 4 + k] = jnp.concatenate(
                [
                    states[g][4 * k : 4 * k + 4, :], hi[:, lanes], mid[:, lanes], low[:, lanes],
                    jnp.zeros((1, LANES), F32),
                ],
                0,
            ).astype(BF16)


def run_mixer(position, step_low, step_proj, step_bias, channels, decay_log, state_maps, begun=None):
    blocked = (TOK // BLK, BLK, CW)
    whole = jax.ShapeDtypeStruct((TOK // BLK, BLK, CH), F32)
    out_map = (TOK // BLK, 2 * BLK, BLK * NS)
    first = begun is None
    if first:
        chunk = lambda i, pos: 0
    else:
        chunk = lambda i, pos: jnp.where(lax.rem(pos[0], 2) == 0, jnp.maximum(i, 1), i)
    fixed = lambda shape: pl.BlockSpec(shape, lambda i, pos: (0,) * len(shape))
    out_specs = [
        pl.BlockSpec(blocked, lambda i, pos: (0, 0, chunk(i, pos))),
        pl.BlockSpec(blocked, lambda i, pos: (0, 0, chunk(i, pos))),
        pl.BlockSpec((CW // LANES * 4, 8, LANES), lambda i, pos: (chunk(i, pos), 0, 0)),
    ]
    out_shape = [whole, whole, jax.ShapeDtypeStruct((N_CTX, 8, LANES), BF16)]
    scratch = [
        pltpu.VMEM(blocked, F32),
        pltpu.VMEM(blocked, F32),
        pltpu.VMEM((TOK, NS, LANES), F32),
    ]
    if first:
        scratch = [pltpu.VMEM(out_map, BF16)] + scratch
    else:
        out_specs = out_specs + [fixed(out_map)]
        out_shape = out_shape + [jax.ShapeDtypeStruct(out_map, BF16)]
    return pl.pallas_call(
        mixer_first_kernel if first else mixer_rest_kernel,
        grid_spec=pltpu.PrefetchScalarGridSpec(
            num_scalar_prefetch=1,
            grid=(1 if first else CH // CW,),
            in_specs=[
                fixed((TOK, 128)),
                pl.BlockSpec((128, CW), lambda i, pos: (0, chunk(i, pos))),
                pl.BlockSpec((1, CW), lambda i, pos: (0, chunk(i, pos))),
                pl.BlockSpec((TOK, CW), lambda i, pos: (0, chunk(i, pos))),
                pl.BlockSpec((NS, CW), lambda i, pos: (0, chunk(i, pos))),
                fixed((2, NS, TOK)),
            ]
            + ([] if first else [pl.BlockSpec(memory_space=pl.ANY)] * 3),
            out_specs=out_specs,
            scratch_shapes=scratch,
        ),
        out_shape=out_shape,
        input_output_aliases={} if first else {7: 0, 8: 1, 9: 2},
        cost_estimate=pl.CostEstimate(
            flops=(1 if first else 5) * 1_000_000_000, bytes_accessed=8 << 20, transcendentals=8 << 20
        ),
        name="mixer_first" if first else "mixer_rest",
    )(
        position, step_low, step_proj, step_bias.reshape(1, CH), channels, decay_log, state_maps,
        *(begun or ()),
    )


def prefix_kernel(pos_ref, got_ref, log_ref, out_ref):
    part = lax.rem(pos_ref[0], 4)
    rates = -jnp.exp(log_ref[...]) * LOG2E
    rate = rates[0:4]
    for k in range(1, 4):
        rate = jnp.where(part == k, rates[4 * k : 4 * k + 4], rate)
    state = jnp.zeros((4, LANES), F32)
    for s in range(N_CTX):
        out_ref[s] = state
        got = got_ref[s].astype(F32)
        total = got[4:5] + got[5:6] + got[6:7]
        state = jnp.exp2(rate * total) * state + got[0:4]


def run_prefix(position, got, decay_log):
    return pl.pallas_call(
        prefix_kernel,
        grid_spec=pltpu.PrefetchScalarGridSpec(
            num_scalar_prefetch=1,
            grid=(1,),
            in_specs=[
                pl.BlockSpec((N_CTX, 8, LANES), lambda i, pos: (0, 0, 0)),
                pl.BlockSpec((NS, LANES), lambda i, pos: (0, pos[0] // 4)),
            ],
            out_specs=pl.BlockSpec((N_CTX, 4, LANES), lambda i, pos: (0, 0, 0)),
        ),
        out_shape=jax.ShapeDtypeStruct((N_CTX, 4, LANES), F32),
        cost_estimate=pl.CostEstimate(flops=1 << 20, bytes_accessed=1 << 18, transcendentals=1 << 15),
        compiler_params=pltpu.CompilerParams(vmem_limit_bytes=8 << 20),
        name="prefix",
    )(position, got, decay_log)


def enter_kernel(
    y_ref, cum_ref, enter_ref, log_ref, out_ref, weight_ref, own_ref, back_ref, o_ref, total_s,
):
    groups = CW // LANES
    i = pl.program_id(0)
    rate = -jnp.exp(log_ref[...]) * LOG2E
    rates = [rate[:, g * LANES : (g + 1) * LANES] for g in range(groups)]
    enter = [
        jnp.concatenate([enter_ref[(i * groups + g) * 4 + k] for k in range(4)], 0)
        for g in range(groups)
    ]

    def block(j, carry):
        past = []
        for t in range(BLK):
            now = []
            for g in range(groups):
                lanes = slice(g * LANES, (g + 1) * LANES)
                decay = jnp.exp2(cum_ref[j, t : t + 1, lanes] * rates[g])
                now.append((decay * enter[g]).astype(BF16))
            past.append(jnp.concatenate(now, 1))
        both = dot(out_ref[j], jnp.concatenate(past, 0))
        rows = pl.ds(pl.multiple_of(j * BLK, BLK), BLK)
        total_s[i, rows, :] = y_ref[j] + both[:BLK, :] + both[BLK:, :]
        return carry

    lax.fori_loop(0, TOK // BLK, block, 0, unroll=4)

    @pl.when(i == CH // CW - 1)
    def _():
        square = jnp.zeros((TOK, LANES), F32)
        for k in range(CH // CW):
            for g in range(groups):
                piece = total_s[k, :, g * LANES : (g + 1) * LANES]
                square += piece * piece
        inverse = lax.rsqrt(jnp.sum(square, -1, keepdims=True) * (1.0 / CH) + 1e-05)
        combined = jnp.transpose(own_ref[...] + back_ref[...].astype(F32))
        for k in range(CH // CW):
            combined += dot((total_s[k] * inverse).astype(BF16), weight_ref[k * CW : (k + 1) * CW, :])
        mean = jnp.mean(combined * combined, -1, keepdims=True)
        o_ref[...] = (combined * lax.rsqrt(mean + 1e-06)).astype(BF16)


def run_enter(y, cum, enter, decay_log, out_map, mixer_weight, own, back):
    blocked = pl.BlockSpec((TOK // BLK, BLK, CW), lambda i: (0, 0, i))
    far = lambda x: pltpu.with_memory_space_constraint(x, pltpu.HBM)
    fixed = lambda shape: pl.BlockSpec(shape, lambda i: (0,) * len(shape))
    return pl.pallas_call(
        enter_kernel,
        grid=(CH // CW,),
        in_specs=[
            blocked,
            blocked,
            VMEM,
            pl.BlockSpec((NS, CW), lambda i: (0, i)),
            fixed((TOK // BLK, 2 * BLK, BLK * NS)),
            fixed((CH, EMB)),
            VMEM,
            VMEM,
        ],
        out_specs=fixed((TOK, EMB)),
        out_shape=jax.ShapeDtypeStruct((TOK, EMB), BF16),
        scratch_shapes=[pltpu.VMEM((CH // CW, TOK, CW), F32)],
        cost_estimate=pl.CostEstimate(
            flops=4_000_000_000, bytes_accessed=6 << 20, transcendentals=8 << 20
        ),
        compiler_params=pltpu.CompilerParams(vmem_limit_bytes=20 << 20),
        name="enter",
    )(far(y), far(cum), enter, far(decay_log), far(out_map), far(mixer_weight), own, back)


def scores_kernel(
    pos_ref, q_ref, p_ref, k0_ref, k1_ref, k2_ref, own_ref, other_ref, stat_ref, raw, w_ref, sems,
):
    def out(h):
        mine = w_ref.at[h, pl.ds(0, 3 * TOK), :]
        other = w_ref.at[h, pl.ds(3 * TOK, 2 * TOK), :]
        return (
            pltpu.make_async_copy(mine, own_ref.at[h], sems.at[0, h]),
            pltpu.make_async_copy(other, other_ref.at[h], sems.at[1, h]),
        )

    def head(h, carry):
        scores_head(h, pos_ref, q_ref, p_ref, k0_ref, k1_ref, k2_ref, w_ref, stat_ref, raw)
        for copy in out(h):
            copy.start()
        return carry

    lax.fori_loop(0, HEADS, head, 0)
    for h in range(HEADS):
        for copy in out(h):
            copy.wait()


def scores_head(h, pos_ref, q_ref, p_ref, k0_ref, k1_ref, k2_ref, w_ref, stat_ref, raw):
    span = pl.ds(pl.multiple_of(h * HD, HD), HD)
    side = lax.rem(pos_ref[0], 2)
    pair = pos_ref[0] // 2
    gone1 = jnp.where(pair >= 1, 0.0, -1e30).astype(F32)
    gone2 = jnp.where(pair >= 2, 0.0, -1e30).astype(F32)
    key = lax.broadcasted_iota(jnp.int32, (HD, HD), 0)
    asker = lax.broadcasted_iota(jnp.int32, (HD, HD), 1)
    line = lax.broadcasted_iota(jnp.int32, (4 * HEADS, TOK), 0)
    k0, k1, k2 = k0_ref[:, span], k1_ref[:, span], k2_ref[:, span]
    zero = jnp.zeros((HD, HD), BF16)

    def weigh(first, kinds, gone, slot):
        tops, sums = [], []
        for side_q in range(2):
            lanes = slice(side_q * HD, (side_q + 1) * HD)

            def load(n, side_k):
                at = (first + n) * TOK + side_k * HD
                x = raw[at : at + HD, lanes]
                kind = kinds[n][side_k][side_q]
                if kind == "upto":
                    x = jnp.where(key <= asker, x, -1e30)
                if kind == "after":
                    x = jnp.where(key > asker, x, -1e30)
                return x

            top = None
            for n in range(len(kinds)):
                block = None
                for side_k in range(2):
                    if kinds[n][side_k][side_q] != "none":
                        x = jnp.max(load(n, side_k), 0, keepdims=True)
                        block = x if block is None else jnp.maximum(block, x)
                block = block * SCALE2 + gone[n]
                top = block if top is None else jnp.maximum(top, block)
            total = jnp.zeros((1, HD), F32)
            for n in range(len(kinds)):
                level = top - gone[n]
                for side_k in range(2):
                    at = (first + n) * TOK + side_k * HD
                    if kinds[n][side_k][side_q] == "none":
                        w_ref[h, at : at + HD, lanes] = zero
                        continue
                    terms = jnp.exp2(load(n, side_k) * SCALE2 - level)
                    total += jnp.sum(terms, 0, keepdims=True)
                    w_ref[h, at : at + HD, lanes] = terms.astype(BF16)
            tops.append(top)
            sums.append(total)
        now = jnp.where(line == slot + h, jnp.concatenate(tops, 1), stat_ref[...])
        stat_ref[...] = jnp.where(line == slot + HEADS + h, jnp.concatenate(sums, 1), now)

    q, other = q_ref[:, span], p_ref[:, span]
    for n, k in enumerate((k0, k1, k2)):
        raw[n * TOK : (n + 1) * TOK, :] = dot_t(k, q)
    raw[3 * TOK : 4 * TOK, :] = dot_t(jnp.where(side == 0, k0, k1), other)
    raw[4 * TOK : 5 * TOK, :] = dot_t(jnp.where(side == 0, k1, k2), other)
    every = (("all", "all"), ("all", "all"))
    weigh(
        0,
        ((("upto", "all"), ("none", "upto")), every, (("after", "none"), ("all", "after"))),
        (jnp.float32(0.0), gone1, gone2),
        0,
    )
    weigh(
        3,
        (every, every),
        (jnp.where(side == 0, 0.0, gone1), jnp.where(side == 0, gone1, gone2)),
        2 * HEADS,
    )


def run_scores(position, query, other, k0, k1, k2):
    return pl.pallas_call(
        scores_kernel,
        in_specs=[SMEM] + [VMEM] * 5,
        out_specs=[AWAY, AWAY, VMEM],
        scratch_shapes=[
            pltpu.VMEM((5 * TOK, TOK), F32),
            pltpu.VMEM((HEADS, 5 * TOK, TOK), BF16),
            pltpu.SemaphoreType.DMA((2, HEADS)),
        ],
        out_shape=[
            pltpu.HBM((HEADS, 3 * TOK, TOK), BF16),
            pltpu.HBM((HEADS, 2 * TOK, TOK), BF16),
            jax.ShapeDtypeStruct((4 * HEADS, TOK), F32),
        ],
        compiler_params=pltpu.CompilerParams(vmem_limit_bytes=16 << 20),
        cost_estimate=pl.CostEstimate(
            flops=700_000_000, bytes_accessed=8 << 20, transcendentals=3 << 20
        ),
        name="scores",
    )(position, pltpu.with_memory_space_constraint(query, pltpu.HBM), other, pltpu.with_memory_space_constraint(k0, pltpu.HBM), k1, k2)


def dot_0(a, b):
    return lax.dot_general(a, b, (((0,), (0,)), ((), ())), preferred_element_type=F32)


def values_kernel(
    mine, pos_ref, w_ref, v0_ref, v1_ref, v2_ref, stat_ref, got_ref, weight_ref, o_ref,
    scale_s, sum_s,
):
    side = lax.rem(pos_ref[0], 2)
    at = lambda ref, k: (ref[k * 8 : k * 8 + 8, :], ref[k * 8 + 8 : k * 8 + 16, :])
    (m0, l0), (m1, l1) = at(stat_ref, 0 if mine else 2), at(got_ref, 2 if mine else 0)
    top = jnp.maximum(m0, m1)
    f0 = jnp.exp2(m0 - top)
    scale_s[...] = f0 / (l0 * f0 + l1 * jnp.exp2(m1 - top))
    sum_s[...] = jnp.zeros_like(sum_s)
    line = lax.broadcasted_iota(jnp.int32, (HEADS, TOK), 0)

    def head(h, carry):
        span = pl.ds(pl.multiple_of(h * HD, HD), HD)
        scale = jnp.sum(jnp.where(line == h, scale_s[...], 0.0), 0, keepdims=True)
        v0, v1, v2 = v0_ref[:, span], v1_ref[:, span], v2_ref[:, span]
        w = lambda n: w_ref[h, n * TOK : (n + 1) * TOK, :]
        if mine:
            taken = dot_0(v0, w(0)) + dot_0(v1, w(1)) + dot_0(v2, w(2))
        else:
            taken = dot_0(jnp.where(side == 0, v0, v1), w(0))
            taken += dot_0(jnp.where(side == 0, v1, v2), w(1))
        sum_s[...] += dot_0(weight_ref[span, :], (taken * scale).astype(BF16))
        return carry

    lax.fori_loop(0, HEADS, head, 0)
    o_ref[...] = sum_s[...].astype(o_ref.dtype)


def run_values(mine, position, weights, v0, v1, v2, stats, got, attend_weight):
    return pl.pallas_call(
        functools.partial(values_kernel, mine),
        in_specs=[SMEM] + [VMEM] * 7,
        out_specs=VMEM,
        scratch_shapes=[
            pltpu.VMEM((HEADS, TOK), F32),
            pltpu.VMEM((EMB, TOK), F32),
        ],
        out_shape=jax.ShapeDtypeStruct((EMB, TOK), F32 if mine else BF16),
        compiler_params=pltpu.CompilerParams(vmem_limit_bytes=16 << 20),
        cost_estimate=pl.CostEstimate(
            flops=400_000_000, bytes_accessed=4 << 20, transcendentals=1 << 12
        ),
        name="values_own" if mine else "values_other",
    )(position, weights, v0, v1, v2, stats, got, attend_weight)


def shift(value, steps):
    return lax.ppermute(value, "ctx", [(s, s + steps) for s in range(N_CTX - steps)])


def swap(value):
    return lax.ppermute(value, "ctx", [(s, s ^ 1) for s in range(N_CTX)])


def per_device(
    query_rows, key_rows, value_rows, channels, step_low, step_proj, step_bias, decay_log,
    state_maps, attend_weight, mixer_weight,
):
    position = lax.axis_index("ctx").astype(jnp.int32).reshape(1)
    mixer_args = (
        position, step_low, step_proj, step_bias, channels, decay_log, state_maps
    )
    begun = run_mixer(*mixer_args)
    other = swap(query_rows)
    k1 = shift(key_rows, 2)
    k2 = shift(key_rows, 4)
    v1 = shift(value_rows, 2)
    y, cum, send, out_map = run_mixer(*mixer_args, begun)
    got = lax.all_to_all(send, "ctx", 0, 0, tiled=True)
    w_own, w_other, stats = run_scores(position, query_rows, other, key_rows, k1, k2)
    v2 = shift(value_rows, 4)
    given = run_prefix(position, got, decay_log)
    enter = lax.all_to_all(given, "ctx", 0, 0, tiled=True)
    got_stats = swap(stats)
    blocks = (value_rows, v1, v2, stats, got_stats, attend_weight)
    give = run_values(False, position, w_other, *blocks)
    back = swap(give)
    own = run_values(True, position, w_own, *blocks)
    return run_enter(y, cum, enter, decay_log, out_map, mixer_weight, own, back)


def solution(mesh):
    rows = P(("dp", "ctx"), None)
    return jax.shard_map(
        per_device,
        mesh=mesh,
        in_specs=(rows, rows, rows, rows, rows, P(), P(), P(), P(None, None, ("dp", "ctx")), P(), P()),
        out_specs=rows,
        check_vma=False,
    )
```

```python
import functools
import math

import jax
import jax.numpy as jnp
from jax import lax
from jax.experimental import pallas as pl
from jax.experimental.pallas import tpu as pltpu
from jax.sharding import PartitionSpec as P


HD = 128
HEADS = 8
TOK = 256
NS = 16
CH = 2048
EMB = 128
CW = 512
LANES = 128
BLK = 16
N_CTX = 64
LOG2E = 1.4426950408889634
SCALE2 = LOG2E / math.sqrt(HD)
VMEM = pl.BlockSpec(memory_space=pltpu.VMEM)
SMEM = pl.BlockSpec(memory_space=pltpu.SMEM)
AWAY = pl.BlockSpec(memory_space=pltpu.HBM)
F32 = jnp.float32
BF16 = jnp.bfloat16


def dot(a, b):
    return jnp.dot(a, b, preferred_element_type=F32)


def dot_t(a, b):
    return lax.dot_general(a, b, (((1,), (1,)), ((), ())), preferred_element_type=F32)


def pieces(x):
    hi = x.astype(BF16)
    rest = x - hi.astype(F32)
    mid = rest.astype(BF16)
    low = (rest - mid.astype(F32)).astype(BF16)
    return hi, mid, low


def softplus(v):
    return jnp.maximum(v, 0.0) + jnp.log1p(jnp.exp(-jnp.abs(v)))


def mixer_kernel(
    low_ref, proj_ref, bias_ref, chan_ref, log_ref, maps_ref,
    y_ref, cum_ref, send_ref, out_ref,
    step_s, flow_s, in_s,
):
    groups = CW // LANES

    @pl.when(pl.program_id(0) == 0)
    def _():
        in_map = maps_ref[0]
        for t in range(TOK):
            in_s[t] = jnp.broadcast_to(in_map[:, t : t + 1], (NS, LANES))
        spread = (
            lax.broadcasted_iota(jnp.int32, (NS, BLK * NS), 1) % NS
            == lax.broadcasted_iota(jnp.int32, (NS, BLK * NS), 0)
        ).astype(F32).astype(BF16)
        keep = (
            lax.broadcasted_iota(jnp.int32, (TOK, BLK * NS), 1) // NS
            == lax.broadcasted_iota(jnp.int32, (TOK, BLK * NS), 0) % BLK
        )
        hi, mid, _ = pieces(jnp.transpose(maps_ref[1]))
        for k, piece in enumerate((hi, mid)):
            rows = jnp.where(keep, dot(piece, spread), 0.0).astype(BF16)
            out_ref[:, k * BLK : (k + 1) * BLK, :] = rows.reshape(TOK // BLK, BLK, BLK * NS)

    rows = 64
    part = rows // BLK
    half = 2 * LANES
    shape = (rows, 2 * rows)
    triangle = (
        lax.broadcasted_iota(jnp.int32, shape, 0)
        >= lax.broadcasted_iota(jnp.int32, shape, 1) % rows
    ).astype(F32).astype(BF16)
    totals = []
    for c in range(CW // half):
        lanes = slice(c * half, (c + 1) * half)
        carry = jnp.zeros((1, half), F32)
        for r in range(TOK // rows):
            at = slice(r * rows, (r + 1) * rows)
            step = softplus(dot(low_ref[at, :], proj_ref[:, lanes]) + bias_ref[:, lanes])
            to = slice(r * part, (r + 1) * part)
            step_s[to, :, lanes] = step.reshape(part, BLK, half)
            flow = step * chan_ref[at, lanes].astype(F32)
            flow_s[to, :, lanes] = flow.reshape(part, BLK, half)
            hi, mid, _ = pieces(step)
            cum = dot(triangle, jnp.concatenate([hi, mid], 0)) + carry
            cum_ref[to, :, lanes] = cum.reshape(part, BLK, half)
            carry = cum[rows - 1 : rows, :]
        totals.append(carry)

    rate = -jnp.exp(log_ref[...]) * LOG2E
    rates = [rate[:, g * LANES : (g + 1) * LANES] for g in range(groups)]

    def block(j, states):
        states = list(states)
        past = []
        for t in range(BLK):
            gain = in_s[j * BLK + t]
            now = []
            for g in range(groups):
                lanes = slice(g * LANES, (g + 1) * LANES)
                decay = jnp.exp2(step_s[j, t : t + 1, lanes] * rates[g])
                states[g] = decay * states[g] + gain * flow_s[j, t : t + 1, lanes]
                now.append(states[g].astype(BF16))
            past.append(jnp.concatenate(now, 1))
        both = dot(out_ref[j], jnp.concatenate(past, 0))
        y_ref[j] = both[:BLK, :] + both[BLK:, :]
        return tuple(states)

    states = lax.fori_loop(
        0, TOK // BLK, block, tuple(jnp.zeros((NS, LANES), F32) for _ in range(groups)), unroll=4
    )
    total = jnp.concatenate(totals, 1)
    hi, mid, low = (v.astype(F32) for v in pieces(total))
    for g in range(groups):
        lanes = slice(g * LANES, (g + 1) * LANES)
        for k in range(NS // 4):
            send_ref[g * 4 + k] = jnp.concatenate(
                [
                    states[g][4 * k : 4 * k + 4, :], hi[:, lanes], mid[:, lanes], low[:, lanes],
                    jnp.zeros((1, LANES), F32),
                ],
                0,
            ).astype(BF16)


def run_mixer(step_low, step_proj, step_bias, channels, decay_log, state_maps):
    blocked = (TOK // BLK, BLK, CW)
    whole = jax.ShapeDtypeStruct((TOK // BLK, BLK, CH), F32)
    out_map = (TOK // BLK, 2 * BLK, BLK * NS)
    fixed = lambda shape: pl.BlockSpec(shape, lambda i: (0,) * len(shape))
    return pl.pallas_call(
        mixer_kernel,
        grid=(CH // CW,),
        in_specs=[
            fixed((TOK, 128)),
            pl.BlockSpec((128, CW), lambda i: (0, i)),
            pl.BlockSpec((1, CW), lambda i: (0, i)),
            pl.BlockSpec((TOK, CW), lambda i: (0, i)),
            pl.BlockSpec((NS, CW), lambda i: (0, i)),
            fixed((2, NS, TOK)),
        ],
        out_specs=[
            pl.BlockSpec(blocked, lambda i: (0, 0, i)),
            pl.BlockSpec(blocked, lambda i: (0, 0, i)),
            pl.BlockSpec((CW // LANES * 4, 8, LANES), lambda i: (i, 0, 0)),
            fixed(out_map),
        ],
        out_shape=[
            whole, whole, jax.ShapeDtypeStruct((N_CTX, 8, LANES), BF16),
            jax.ShapeDtypeStruct(out_map, BF16),
        ],
        scratch_shapes=[
            pltpu.VMEM(blocked, F32),
            pltpu.VMEM(blocked, F32),
            pltpu.VMEM((TOK, NS, LANES), F32),
        ],
        cost_estimate=pl.CostEstimate(
            flops=6_000_000_000, bytes_accessed=8 << 20, transcendentals=8 << 20
        ),
        name="mixer",
    )(step_low, step_proj, step_bias.reshape(1, CH), channels, decay_log, state_maps)


def prefix_kernel(pos_ref, got_ref, log_ref, out_ref):
    part = lax.rem(pos_ref[0], 4)
    rates = -jnp.exp(log_ref[...]) * LOG2E
    rate = rates[0:4]
    for k in range(1, 4):
        rate = jnp.where(part == k, rates[4 * k : 4 * k + 4], rate)
    state = jnp.zeros((4, LANES), F32)
    for s in range(N_CTX):
        out_ref[s] = state
        got = got_ref[s].astype(F32)
        total = got[4:5] + got[5:6] + got[6:7]
        state = jnp.exp2(rate * total) * state + got[0:4]


def run_prefix(position, got, decay_log):
    return pl.pallas_call(
        prefix_kernel,
        grid_spec=pltpu.PrefetchScalarGridSpec(
            num_scalar_prefetch=1,
            grid=(1,),
            in_specs=[
                pl.BlockSpec((N_CTX, 8, LANES), lambda i, pos: (0, 0, 0)),
                pl.BlockSpec((NS, LANES), lambda i, pos: (0, pos[0] // 4)),
            ],
            out_specs=pl.BlockSpec((N_CTX, 4, LANES), lambda i, pos: (0, 0, 0)),
        ),
        out_shape=jax.ShapeDtypeStruct((N_CTX, 4, LANES), F32),
        cost_estimate=pl.CostEstimate(flops=1 << 20, bytes_accessed=1 << 18, transcendentals=1 << 15),
        compiler_params=pltpu.CompilerParams(vmem_limit_bytes=8 << 20),
        name="prefix",
    )(position, got, decay_log)


def enter_kernel(
    y_ref, cum_ref, enter_ref, log_ref, out_ref, weight_ref, own_ref, back_ref, o_ref, total_s,
):
    groups = CW // LANES
    i = pl.program_id(0)
    rate = -jnp.exp(log_ref[...]) * LOG2E
    rates = [rate[:, g * LANES : (g + 1) * LANES] for g in range(groups)]
    enter = [
        jnp.concatenate([enter_ref[(i * groups + g) * 4 + k] for k in range(4)], 0)
        for g in range(groups)
    ]

    def block(j, carry):
        past = []
        for t in range(BLK):
            now = []
            for g in range(groups):
                lanes = slice(g * LANES, (g + 1) * LANES)
                decay = jnp.exp2(cum_ref[j, t : t + 1, lanes] * rates[g])
                now.append((decay * enter[g]).astype(BF16))
            past.append(jnp.concatenate(now, 1))
        both = dot(out_ref[j], jnp.concatenate(past, 0))
        rows = pl.ds(pl.multiple_of(j * BLK, BLK), BLK)
        total_s[i, rows, :] = y_ref[j] + both[:BLK, :] + both[BLK:, :]
        return carry

    lax.fori_loop(0, TOK // BLK, block, 0, unroll=4)

    @pl.when(i == CH // CW - 1)
    def _():
        square = jnp.zeros((TOK, LANES), F32)
        for k in range(CH // CW):
            for g in range(groups):
                piece = total_s[k, :, g * LANES : (g + 1) * LANES]
                square += piece * piece
        inverse = lax.rsqrt(jnp.sum(square, -1, keepdims=True) * (1.0 / CH) + 1e-05)
        combined = jnp.transpose(own_ref[...] + back_ref[...].astype(F32))
        for k in range(CH // CW):
            combined += dot((total_s[k] * inverse).astype(BF16), weight_ref[k * CW : (k + 1) * CW, :])
        mean = jnp.mean(combined * combined, -1, keepdims=True)
        o_ref[...] = (combined * lax.rsqrt(mean + 1e-06)).astype(BF16)


def run_enter(y, cum, enter, decay_log, out_map, mixer_weight, own, back):
    blocked = pl.BlockSpec((TOK // BLK, BLK, CW), lambda i: (0, 0, i))
    far = lambda x: pltpu.with_memory_space_constraint(x, pltpu.HBM)
    fixed = lambda shape: pl.BlockSpec(shape, lambda i: (0,) * len(shape))
    return pl.pallas_call(
        enter_kernel,
        grid=(CH // CW,),
        in_specs=[
            blocked,
            blocked,
            VMEM,
            pl.BlockSpec((NS, CW), lambda i: (0, i)),
            fixed((TOK // BLK, 2 * BLK, BLK * NS)),
            fixed((CH, EMB)),
            VMEM,
            VMEM,
        ],
        out_specs=fixed((TOK, EMB)),
        out_shape=jax.ShapeDtypeStruct((TOK, EMB), BF16),
        scratch_shapes=[pltpu.VMEM((CH // CW, TOK, CW), F32)],
        cost_estimate=pl.CostEstimate(
            flops=4_000_000_000, bytes_accessed=6 << 20, transcendentals=8 << 20
        ),
        compiler_params=pltpu.CompilerParams(vmem_limit_bytes=20 << 20),
        name="enter",
    )(far(y), far(cum), enter, far(decay_log), far(out_map), far(mixer_weight), own, back)


def scores_kernel(
    pos_ref, q_ref, p_ref, k0_ref, k1_ref, k2_ref, own_ref, other_ref, stat_ref, raw, w_ref, sems,
):
    def out(h):
        mine = w_ref.at[h, pl.ds(0, 3 * TOK), :]
        other = w_ref.at[h, pl.ds(3 * TOK, 2 * TOK), :]
        return (
            pltpu.make_async_copy(mine, own_ref.at[h], sems.at[0, h]),
            pltpu.make_async_copy(other, other_ref.at[h], sems.at[1, h]),
        )

    def head(h, carry):
        scores_head(h, pos_ref, q_ref, p_ref, k0_ref, k1_ref, k2_ref, w_ref, stat_ref, raw)
        for copy in out(h):
            copy.start()
        return carry

    lax.fori_loop(0, HEADS, head, 0)
    for h in range(HEADS):
        for copy in out(h):
            copy.wait()


def scores_head(h, pos_ref, q_ref, p_ref, k0_ref, k1_ref, k2_ref, w_ref, stat_ref, raw):
    span = pl.ds(pl.multiple_of(h * HD, HD), HD)
    side = lax.rem(pos_ref[0], 2)
    pair = pos_ref[0] // 2
    gone1 = jnp.where(pair >= 1, 0.0, -1e30).astype(F32)
    gone2 = jnp.where(pair >= 2, 0.0, -1e30).astype(F32)
    key = lax.broadcasted_iota(jnp.int32, (HD, HD), 0)
    asker = lax.broadcasted_iota(jnp.int32, (HD, HD), 1)
    line = lax.broadcasted_iota(jnp.int32, (4 * HEADS, TOK), 0)
    k0, k1, k2 = k0_ref[:, span], k1_ref[:, span], k2_ref[:, span]
    zero = jnp.zeros((HD, HD), BF16)

    def weigh(first, kinds, gone, slot):
        tops, sums = [], []
        for side_q in range(2):
            lanes = slice(side_q * HD, (side_q + 1) * HD)

            def load(n, side_k):
                at = (first + n) * TOK + side_k * HD
                x = raw[at : at + HD, lanes]
                kind = kinds[n][side_k][side_q]
                if kind == "upto":
                    x = jnp.where(key <= asker, x, -1e30)
                if kind == "after":
                    x = jnp.where(key > asker, x, -1e30)
                return x

            top = None
            for n in range(len(kinds)):
                block = None
                for side_k in range(2):
                    if kinds[n][side_k][side_q] != "none":
                        x = jnp.max(load(n, side_k), 0, keepdims=True)
                        block = x if block is None else jnp.maximum(block, x)
                block = block * SCALE2 + gone[n]
                top = block if top is None else jnp.maximum(top, block)
            total = jnp.zeros((1, HD), F32)
            for n in range(len(kinds)):
                level = top - gone[n]
                for side_k in range(2):
                    at = (first + n) * TOK + side_k * HD
                    if kinds[n][side_k][side_q] == "none":
                        w_ref[h, at : at + HD, lanes] = zero
                        continue
                    terms = jnp.exp2(load(n, side_k) * SCALE2 - level)
                    total += jnp.sum(terms, 0, keepdims=True)
                    w_ref[h, at : at + HD, lanes] = terms.astype(BF16)
            tops.append(top)
            sums.append(total)
        now = jnp.where(line == slot + h, jnp.concatenate(tops, 1), stat_ref[...])
        stat_ref[...] = jnp.where(line == slot + HEADS + h, jnp.concatenate(sums, 1), now)

    q, other = q_ref[:, span], p_ref[:, span]
    for n, k in enumerate((k0, k1, k2)):
        raw[n * TOK : (n + 1) * TOK, :] = dot_t(k, q)
    raw[3 * TOK : 4 * TOK, :] = dot_t(jnp.where(side == 0, k0, k1), other)
    raw[4 * TOK : 5 * TOK, :] = dot_t(jnp.where(side == 0, k1, k2), other)
    every = (("all", "all"), ("all", "all"))
    weigh(
        0,
        ((("upto", "all"), ("none", "upto")), every, (("after", "none"), ("all", "after"))),
        (jnp.float32(0.0), gone1, gone2),
        0,
    )
    weigh(
        3,
        (every, every),
        (jnp.where(side == 0, 0.0, gone1), jnp.where(side == 0, gone1, gone2)),
        2 * HEADS,
    )


def run_scores(position, query, other, k0, k1, k2):
    return pl.pallas_call(
        scores_kernel,
        in_specs=[SMEM] + [VMEM] * 5,
        out_specs=[AWAY, AWAY, VMEM],
        scratch_shapes=[
            pltpu.VMEM((5 * TOK, TOK), F32),
            pltpu.VMEM((HEADS, 5 * TOK, TOK), BF16),
            pltpu.SemaphoreType.DMA((2, HEADS)),
        ],
        out_shape=[
            pltpu.HBM((HEADS, 3 * TOK, TOK), BF16),
            pltpu.HBM((HEADS, 2 * TOK, TOK), BF16),
            jax.ShapeDtypeStruct((4 * HEADS, TOK), F32),
        ],
        compiler_params=pltpu.CompilerParams(vmem_limit_bytes=16 << 20),
        cost_estimate=pl.CostEstimate(
            flops=700_000_000, bytes_accessed=8 << 20, transcendentals=3 << 20
        ),
        name="scores",
    )(position, pltpu.with_memory_space_constraint(query, pltpu.HBM), other, pltpu.with_memory_space_constraint(k0, pltpu.HBM), k1, k2)


def dot_0(a, b):
    return lax.dot_general(a, b, (((0,), (0,)), ((), ())), preferred_element_type=F32)


def values_kernel(
    mine, pos_ref, w_ref, v0_ref, v1_ref, v2_ref, stat_ref, got_ref, weight_ref, o_ref,
    scale_s, sum_s,
):
    side = lax.rem(pos_ref[0], 2)
    at = lambda ref, k: (ref[k * 8 : k * 8 + 8, :], ref[k * 8 + 8 : k * 8 + 16, :])
    (m0, l0), (m1, l1) = at(stat_ref, 0 if mine else 2), at(got_ref, 2 if mine else 0)
    top = jnp.maximum(m0, m1)
    f0 = jnp.exp2(m0 - top)
    scale_s[...] = f0 / (l0 * f0 + l1 * jnp.exp2(m1 - top))
    sum_s[...] = jnp.zeros_like(sum_s)
    line = lax.broadcasted_iota(jnp.int32, (HEADS, TOK), 0)

    def head(h, carry):
        span = pl.ds(pl.multiple_of(h * HD, HD), HD)
        scale = jnp.sum(jnp.where(line == h, scale_s[...], 0.0), 0, keepdims=True)
        v0, v1, v2 = v0_ref[:, span], v1_ref[:, span], v2_ref[:, span]
        w = lambda n: w_ref[h, n * TOK : (n + 1) * TOK, :]
        if mine:
            taken = dot_0(v0, w(0)) + dot_0(v1, w(1)) + dot_0(v2, w(2))
        else:
            taken = dot_0(jnp.where(side == 0, v0, v1), w(0))
            taken += dot_0(jnp.where(side == 0, v1, v2), w(1))
        sum_s[...] += dot_0(weight_ref[span, :], (taken * scale).astype(BF16))
        return carry

    lax.fori_loop(0, HEADS, head, 0, unroll=4)
    o_ref[...] = sum_s[...].astype(o_ref.dtype)


def run_values(mine, position, weights, v0, v1, v2, stats, got, attend_weight):
    return pl.pallas_call(
        functools.partial(values_kernel, mine),
        in_specs=[SMEM] + [VMEM] * 7,
        out_specs=VMEM,
        scratch_shapes=[
            pltpu.VMEM((HEADS, TOK), F32),
            pltpu.VMEM((EMB, TOK), F32),
        ],
        out_shape=jax.ShapeDtypeStruct((EMB, TOK), F32 if mine else BF16),
        compiler_params=pltpu.CompilerParams(vmem_limit_bytes=16 << 20),
        cost_estimate=pl.CostEstimate(
            flops=400_000_000, bytes_accessed=4 << 20, transcendentals=1 << 12
        ),
        name="values_own" if mine else "values_other",
    )(position, weights, v0, v1, v2, stats, got, attend_weight)


def shift(value, steps):
    return lax.ppermute(value, "ctx", [(s, s + steps) for s in range(N_CTX - steps)])


def swap(value):
    return lax.ppermute(value, "ctx", [(s, s ^ 1) for s in range(N_CTX)])


def per_device(
    query_rows, key_rows, value_rows, channels, step_low, step_proj, step_bias, decay_log,
    state_maps, attend_weight, mixer_weight,
):
    position = lax.axis_index("ctx").astype(jnp.int32).reshape(1)
    other = swap(query_rows)
    k1 = shift(key_rows, 2)
    k2 = shift(key_rows, 4)
    v1 = shift(value_rows, 2)
    y, cum, send, out_map = run_mixer(
        step_low, step_proj, step_bias, channels, decay_log, state_maps
    )
    got = lax.all_to_all(send, "ctx", 0, 0, tiled=True)
    w_own, w_other, stats = run_scores(position, query_rows, other, key_rows, k1, k2)
    v2 = shift(value_rows, 4)
    given = run_prefix(position, got, decay_log)
    enter = lax.all_to_all(given, "ctx", 0, 0, tiled=True)
    got_stats = swap(stats)
    blocks = (value_rows, v1, v2, stats, got_stats, attend_weight)
    give = run_values(False, position, w_other, *blocks)
    back = swap(give)
    own = run_values(True, position, w_own, *blocks)
    return run_enter(y, cum, enter, decay_log, out_map, mixer_weight, own, back)


def solution(mesh):
    rows = P(("dp", "ctx"), None)
    return jax.shard_map(
        per_device,
        mesh=mesh,
        in_specs=(rows, rows, rows, rows, rows, P(), P(), P(), P(None, None, ("dp", "ctx")), P(), P()),
        out_specs=rows,
        check_vma=False,
    )
```
